32 devices in a mesh: groups: 2 (over y), frame: 4 (over z), row: 2 (over core), head: 2 (over x).
Axes of the slice: x: 2, y: 2, z: 4, core: 2. Of those that a mesh axis runs over, the one named last changes fastest.
Arguments:
- queries: bfloat16 [8, 16, 48, 768], P(('groups', 'frame'), 'row', None, 'head'), parts along dimension 0, may hold values from -8 to 8
- keys: bfloat16 [8, 16, 48, 768], P(('groups', 'frame'), 'row', None, 'head'), parts along dimension 0, may hold values from -8 to 8
- values: bfloat16 [8, 16, 48, 768], P(('groups', 'frame'), 'row', None, 'head'), parts along dimension 0, may hold values from -6 to 6
- valid_prev: int32 [8, 16], P(('groups', 'frame'), 'row'), parts along dimension 0, may hold values 0 or 1
- mem_index: int32 [4], P('groups'), parts along dimension 0, may hold values from 0 to 3
Outputs:
- attended: bfloat16 [8, 16, 48, 768], P(('groups', 'frame'), 'row', None, 'head'), parts along dimension 0
The draws below stay inside these ranges and needn't reach their ends.
There are 2 independent parts, one for each index of `groups`. The reference program is written for one: setup_inputs(seed, part) draws one part's arguments, and reference() takes and returns one part's arrays. A program takes and returns all parts, laid end to end along the dimension named above; each array names one. Nothing has to cross between parts.
All inputs are finite; a program needn't handle non-finite values. No bound on the sum of `valid_prev` on one device may be relied on, other than what follows from the above.
Results may differ from the reference program's by a relative error of at most 0.0085.
Values may be sent and summed in bfloat16 or wider, within the bound.
No kernel may reach another device: no remote copies, remote signals or barrier semaphores. Data moves between devices by JAX's collectives and lax.ppermute only.
A program may use at most 128 MiB of HBM per device.

```python
import jax
import jax.numpy as jnp
from jax import lax

HEAD_DIM = 128
FW = 48
WINDOW = 2
MEMORY = 2
HEADS = 6
FRAMES = 4
FH = 16


def drawn_fields(key):
    base = jax.random.fold_in(key, 11)
    query_key, keys_key = jax.random.split(base, 2)
    shape = (FRAMES, FH, FW, HEADS * HEAD_DIM)
    query_field = 2.5 * jax.random.truncated_normal(query_key, -3.2, 3.2, shape)
    keys_field = jax.random.truncated_normal(keys_key, -6.0, 6.0, shape)
    return (query_field, keys_field)


def draw_queries(key, part):
    return drawn_fields(key)[0].astype(jnp.bfloat16)


def draw_keys(key, part):
    return drawn_fields(key)[1].astype(jnp.bfloat16)


def touch_ends(values, stream_key, low, largest):
    extent = values.shape
    spot = [jax.random.randint(jax.random.fold_in(stream_key, axis), (), 0, extent[axis]) for axis in range(len(extent))]
    values = values.at[tuple(spot)].set(low)
    longest = extent.index(max(extent))
    spot[longest] = (spot[longest] + 1) % extent[longest]
    return values.at[tuple(spot)].set(largest)


def block_levels(stream_key, extent, shards, low, top_value):
    factor_of = 1.0
    for position, blocks in shards:
        steps = jax.random.uniform(jax.random.fold_in(jax.random.fold_in(stream_key, 6), position), (blocks,), jnp.float32, low / len(shards), top_value / len(shards))
        factor_of = factor_of * jnp.repeat(jnp.exp(steps), extent[position] // blocks).reshape((-1,) + (1,) * (len(extent) - 1 - position))
    return factor_of


def gaussian(own_key, extent, width, most, pieces=(), held_as=jnp.bfloat16):
    values = jax.random.normal(own_key, extent, jnp.float32) * width
    if len(pieces) > 0:
        values = block_levels(own_key, extent, pieces, -0.22, 0.18) * values
    return jnp.clip(values, min=-most, max=most).astype(held_as)


def setup_inputs(seed: int = 0, part: int = 0) -> dict:
    key_list = jax.random.split(jax.random.key(seed), 6)
    part_splits = jax.random.split(jax.random.fold_in(key_list[5], part), 6)
    queries = draw_queries(jax.random.fold_in(jax.random.fold_in(key_list[5], part), 71), part)
    keys = draw_keys(jax.random.fold_in(jax.random.fold_in(key_list[5], part), 71), part)
    values = gaussian(part_splits[2], (FRAMES, FH, FW, HEADS * HEAD_DIM), 1.0, 6.0, ((0, 4), (1, 2), (3, 2)))
    valid_prev = touch_ends((jax.random.randint(part_splits[3], (FRAMES, FH), 0, 2) < 1).astype(jnp.int32), jax.random.fold_in(part_splits[3], 1), 0, 1)
    mem_index = jax.random.randint(part_splits[4], (MEMORY,), 0, FRAMES).astype(jnp.int32)
    return {"queries": queries, "keys": keys, "values": values, "valid_prev": valid_prev, "mem_index": mem_index}


def reference(queries, keys, values, valid_prev, mem_index):
    frames = queries.shape[0]
    frame_rows = queries.shape[1]
    frame_width = queries.shape[2]
    tokens = frame_rows * frame_width
    head_count = queries.shape[3] // HEAD_DIM

    def by_heads(array):
        return array.reshape(frames, tokens, head_count, HEAD_DIM)

    query_heads = by_heads(queries)
    key_heads = by_heads(keys)
    value_heads = by_heads(values)
    row_index = jnp.arange(tokens, dtype=jnp.int32) // frame_width
    near_rows = jnp.abs(row_index[:, None] - row_index[None, :]) <= WINDOW
    memory_keys = jnp.concatenate([key_heads[mem_index[0]], key_heads[mem_index[1]]], 0)
    memory_values = jnp.concatenate([value_heads[mem_index[0]], value_heads[mem_index[1]]], 0)

    def one_frame(frame_index):
        earlier = jnp.maximum(frame_index - 1, 0)
        row_valid = jnp.repeat(valid_prev[frame_index] > 0, frame_width)
        usable = row_valid & (frame_index > 0)
        key_set = jnp.concatenate([key_heads[frame_index], key_heads[earlier], memory_keys], 0).astype(jnp.float32)
        value_set = jnp.concatenate([value_heads[frame_index], value_heads[earlier], memory_values], 0).astype(jnp.float32)
        allowed = jnp.concatenate([jnp.ones((tokens, tokens), dtype=bool), near_rows & usable[:, None], jnp.ones((tokens, 2 * tokens), dtype=bool)], 1)
        scores = jnp.einsum("qhd,khd->hqk", query_heads[frame_index].astype(jnp.float32), key_set) * (HEAD_DIM ** -0.5)
        scores = jnp.where(allowed[None], scores, -jnp.inf)
        peak = jnp.max(scores, axis=2, keepdims=True)
        exponent = jnp.exp(scores - peak)
        weights = (exponent / jnp.sum(exponent, axis=2, keepdims=True)).astype(jnp.bfloat16)
        result = jnp.einsum("hqk,khd->qhd", weights.astype(jnp.float32), value_set)
        return result.reshape(frame_rows, frame_width, head_count * HEAD_DIM).astype(jnp.bfloat16)

    return lax.map(one_frame, jnp.arange(frames, dtype=jnp.int32))
```

```python
import functools

import jax
import jax.numpy as jnp
from jax import lax
from jax.experimental import pallas as pl
from jax.experimental.pallas import tpu as pltpu
from jax.sharding import PartitionSpec as P

HEAD_DIM = 128
WINDOW = 2
SCALE = HEAD_DIM**-0.5 * 1.4426950408889634
FLOOR = -1e30
BLOCK = 128


def moved(block, axis, pairs):
    return lax.ppermute(block, axis, pairs)


def swapped(block):
    return lax.ppermute(block, "row", [(0, 1), (1, 0)])


def row_dot(a, b):
    return lax.dot_general(a, b, (((1,), (1,)), ((), ())), preferred_element_type=jnp.float32)


def attend_kernel(plan, n_q, n_f, fresh, finish, width, *refs):
    refs = list(refs)
    mem_ref = refs.pop(0)
    valid_refs = [refs.pop(0) for _ in range(n_q)]
    q_refs = [refs.pop(0) for _ in range(n_q)]
    frames = [[refs.pop(0) for _ in range(4)] for _ in range(n_f)]
    states = [None if fresh[i] else (refs.pop(0), refs.pop(0)) for i in range(n_q)]
    outs = [(refs.pop(0),) if finish[i] else (refs.pop(0), refs.pop(0)) for i in range(n_q)]
    acc, stat = refs
    queries = q_refs[0].shape[0]
    rows = queries // width
    band = lax.axis_index("row")
    lane = lax.broadcasted_iota(jnp.int32, (1, HEAD_DIM), 1)

    for i in range(n_q):
        if fresh[i]:
            acc[i] = jnp.zeros_like(acc[i])
            stat[i] = jnp.where(lane == 0, FLOOR, jnp.zeros_like(stat[i]))
        else:
            acc[i] = states[i][0][...]
            stat[i] = states[i][1][...]

    def step(i, f, times, window):
        key_a, value_a, key_b, value_b = frames[f]
        factor = times.astype(jnp.float32)
        for start in range(0, queries, BLOCK):
            part = pl.ds(start, BLOCK)
            query = q_refs[i][part, :]
            scores = [row_dot(query, key[...]) * SCALE for key in (key_a, key_b)]
            if window:
                place = lax.broadcasted_iota(jnp.int32, (BLOCK, 1), 0) + start
                row = jnp.full((BLOCK, 1), -1000, jnp.int32)
                for r in range(rows):
                    here = jnp.where(valid_refs[i][0, r] > 0, band * rows + r, -1000)
                    row = jnp.where((place >= r * width) & (place < (r + 1) * width), here, row)
                place = lax.broadcasted_iota(jnp.int32, (1, queries), 1)
                key_row = jnp.zeros((1, queries), jnp.int32)
                for r in range(1, rows):
                    key_row = key_row + (place >= r * width).astype(jnp.int32)
                near = [
                    jnp.abs(key_row + half * rows - row) <= WINDOW for half in (band, 1 - band)
                ]
                weight = [jnp.where(n, factor + 1.0, factor) for n in near]
                scores = [jnp.where(w > 0.0, s, -jnp.inf) for s, w in zip(scores, weight)]
            old = stat[i, part, 0:1]
            total = stat[i, part, 1:2]
            peak = jnp.maximum(
                jnp.max(scores[0], axis=1, keepdims=True), jnp.max(scores[1], axis=1, keepdims=True)
            )
            peak = jnp.maximum(old, peak)
            terms = [jnp.exp2(s - peak) for s in scores]
            if window:
                terms = [t * w for t, w in zip(terms, weight)]
            added = jnp.sum(terms[0], axis=1, keepdims=True) + jnp.sum(
                terms[1], axis=1, keepdims=True
            )
            mixed = sum(
                jnp.dot(t.astype(jnp.bfloat16), v[...], preferred_element_type=jnp.float32)
                for t, v in zip(terms, (value_a, value_b))
            )
            if not window:
                added = added * factor
                mixed = mixed * factor
            fade = jnp.exp2(old - peak)
            acc[i, part, :] = acc[i, part, :] * fade + mixed
            stat[i, part, :] = jnp.where(lane == 0, peak, total * fade + added)

    z = lax.axis_index("frame")
    for i in range(n_q):
        for f in range(n_f):
            wanted = plan(z, mem_ref[0], mem_ref[1], i, f)
            if wanted is None:
                continue
            times, window = wanted
            if window is None:
                pl.when(times > 0)(functools.partial(step, i, f, times, False))
            else:
                pl.when(window)(functools.partial(step, i, f, times, True))
                pl.when((times > 0) & jnp.logical_not(window))(
                    functools.partial(step, i, f, times, False)
                )

    for i in range(n_q):
        if finish[i]:
            outs[i][0][...] = (acc[i] / stat[i, :, 1:2]).astype(jnp.bfloat16)
        else:
            outs[i][0][...] = acc[i]
            outs[i][1][...] = stat[i]


def attend(plan, mem_index, valids, queries, frames, states, finish, width):
    n_q, n_f = len(queries), len(frames)
    tokens, channels = queries[0].shape
    heads = channels // HEAD_DIM
    block = pl.BlockSpec((tokens, HEAD_DIM), lambda h: (0, h))
    scalars = pl.BlockSpec(memory_space=pltpu.SMEM)
    fresh = tuple(s is None for s in states)
    operands = [mem_index, *valids, *queries]
    specs = [scalars] * (1 + n_q) + [block] * n_q
    for frame in frames:
        operands += frame
        specs += [block] * 4
    for state in states:
        if state is not None:
            operands += state
            specs += [block] * 2
    shapes = []
    for done in finish:
        if done:
            shapes.append(jax.ShapeDtypeStruct((tokens, channels), jnp.bfloat16))
        else:
            shapes += [jax.ShapeDtypeStruct((tokens, channels), jnp.float32)] * 2
    outs = pl.pallas_call(
        functools.partial(attend_kernel, plan, n_q, n_f, fresh, tuple(finish), width),
        grid=(heads,),
        in_specs=specs,
        out_specs=[block] * len(shapes),
        out_shape=shapes,
        scratch_shapes=[
            pltpu.VMEM((n_q, tokens, HEAD_DIM), jnp.float32),
            pltpu.VMEM((n_q, tokens, HEAD_DIM), jnp.float32),
        ],
        compiler_params=pltpu.CompilerParams(vmem_limit_bytes=32 << 20),
        cost_estimate=pl.CostEstimate(
            flops=n_q * n_f * 8 * tokens * tokens * channels,
            transcendentals=n_q * n_f * 2 * tokens * tokens * heads,
            bytes_accessed=(n_f * 4 + n_q * 6) * tokens * channels * 2,
        ),
    )(*operands)
    outs = list(outs)
    return [outs.pop(0) if done else (outs.pop(0), outs.pop(0)) for done in finish]


def plan_four(pairs):
    def plan(z, first, second, i, f):
        query_set, frame = pairs[0][i], pairs[1][f]
        if (query_set, frame) in pairs[2]:
            return None
        middle = (z == 1) | (z == 2)
        ids = (z, 3 - z, 3 * (z - 1), 6 - 3 * z)
        mine = ids[0] if query_set == 0 else ids[2]
        times = (
            (ids[frame] == mine).astype(jnp.int32)
            + (first == ids[frame]).astype(jnp.int32)
            + (second == ids[frame]).astype(jnp.int32)
        )
        times = jnp.where(middle, times, 0)
        if (query_set, frame) in ((0, 1), (0, 2), (1, 0)):
            return times, middle & (ids[frame] == mine - 1)
        return times, None

    return plan


def plan_any(z, first, second, i, f):
    one = jnp.int32(1)
    if f == 1:
        return jnp.int32(0), z > 0
    return one, None


def four_frames(queries, keys, values, valid_prev, mem_index):
    shape = queries.shape
    width = shape[2]
    tokens = shape[1] * width

    def flat(block):
        return block.reshape(tokens, shape[3])

    query, key, value = flat(queries), flat(keys), flat(values)
    inward = [(0, 1), (3, 2)]
    across = [(1, 2), (2, 1)]
    end_key = moved(key, "frame", inward)
    end_value = moved(value, "frame", inward)
    mid_key = moved(key, "frame", across)
    mid_value = moved(value, "frame", across)
    marks = jnp.broadcast_to(valid_prev[0][:, None], (shape[1], shape[3])).astype(jnp.bfloat16)
    marks = jnp.pad(marks, ((0, 16 - shape[1]), (0, 0)))
    end_query = moved(jnp.concatenate([query, marks], 0), "frame", inward)
    far_key = moved(end_key, "frame", across)
    far_value = moved(end_value, "frame", across)
    end_valid = end_query[tokens : tokens + shape[1], 0].astype(jnp.int32)[None]
    end_query = end_query[:tokens]

    def frame(k, v):
        return [k, v, swapped(k), swapped(v)]

    own = frame(key, value)
    mid = frame(mid_key, mid_value)
    end = frame(end_key, end_value)
    far = frame(far_key, far_value)
    (state,) = attend(
        plan_four(((0,), (0,), ())), mem_index, [valid_prev], [query], [own], [None], [False], width
    )
    state, end_state = attend(
        plan_four(((0, 1), (0, 1, 2), ((0, 0),))),
        mem_index,
        [valid_prev, end_valid],
        [query, end_query],
        [own, mid, end],
        [state, None],
        [False, False],
        width,
    )
    (end_out,) = attend(
        plan_four(((1,), (3,), ())),
        mem_index,
        [end_valid],
        [end_query],
        [far],
        [end_state],
        [True],
        width,
    )
    back = moved(end_out, "frame", [(1, 0), (2, 3)])
    (out,) = attend(
        plan_four(((0,), (3,), ())), mem_index, [valid_prev], [query], [far], [state], [True], width
    )
    z = lax.axis_index("frame")
    return jnp.where((z == 1) | (z == 2), out, back).reshape(shape)


def any_frames(queries, keys, values, valid_prev, mem_index):
    shape = queries.shape
    width = shape[2]
    tokens = shape[1] * width
    count = lax.axis_size("frame")
    z = lax.axis_index("frame")

    def flat(block):
        return block.reshape(tokens, shape[3])

    query, key, value = flat(queries), flat(keys), flat(values)
    onward = [(i, i + 1) for i in range(count - 1)]
    prev = [moved(key, "frame", onward), moved(value, "frame", onward)]
    both = jnp.stack([key, value])
    masked = jnp.stack([jnp.where(z == mem_index[s], both, jnp.zeros_like(both)) for s in range(2)])
    memory = lax.psum(masked, "frame")
    frames = []
    for k, v in ((key, value), prev, memory[0], memory[1]):
        frames.append([k, v, swapped(k), swapped(v)])
    (out,) = attend(plan_any, mem_index, [valid_prev], [query], frames, [None], [True], width)
    return out.reshape(shape)


def solution(mesh):
    spread = P(("groups", "frame"), "row", None, "head")
    body = four_frames if mesh.shape["frame"] == 4 else any_frames
    return jax.shard_map(
        body,
        mesh=mesh,
        in_specs=(spread, spread, spread, P(("groups", "frame"), "row"), P("groups")),
        out_specs=spread,
        check_vma=False,
    )
```

```python
import functools

import jax
import jax.numpy as jnp
from jax import lax
from jax.experimental import pallas as pl
from jax.experimental.pallas import tpu as pltpu
from jax.sharding import PartitionSpec as P

HEAD_DIM = 128
WINDOW = 2
SCALE = HEAD_DIM**-0.5 * 1.4426950408889634
FLOOR = -1e30
BLOCK = 128
LOG2_3 = 1.584962500721156


def moved(block, pairs):
    return lax.ppermute(block, "frame", pairs)


def swapped(block):
    return lax.ppermute(block, "row", [(0, 1), (1, 0)])


def log2_weight(count):
    return jnp.where(
        count < 1, -jnp.inf, jnp.where(count < 2, 0.0, jnp.where(count < 3, 1.0, LOG2_3))
    ).astype(jnp.float32)


def attend_kernel(plan, n_q, n_f, fresh, finish, windows, width, *refs):
    refs = list(refs)
    mem_ref = refs.pop(0)
    valid_refs = [refs.pop(0) for _ in range(n_q)]
    q_refs = [refs.pop(0) for _ in range(n_q)]
    frames = [[refs.pop(0) for _ in range(4)] for _ in range(n_f)]
    states = [None if fresh[i] else (refs.pop(0), refs.pop(0)) for i in range(n_q)]
    outs = [(refs.pop(0),) if finish[i] else (refs.pop(0), refs.pop(0)) for i in range(n_q)]
    query_buf, key_buf, value_buf, acc, peaks, sems = refs
    queries, channels = q_refs[0].shape
    heads = channels // HEAD_DIM
    rows = queries // width
    band = lax.axis_index("row")
    z = lax.axis_index("frame")

    copies = []
    for f in range(n_f):
        for half in range(2):
            for part, buf in enumerate((key_buf, value_buf)):
                copies.append(
                    pltpu.make_async_copy(
                        frames[f][2 * half + part],
                        buf.at[f, pl.ds(half * queries, queries), :],
                        sems.at[f, half, part],
                    )
                )
    for i in range(n_q):
        copies.append(pltpu.make_async_copy(q_refs[i], query_buf.at[i], sems.at[n_f + i, 0, 0]))
    for copy in copies:
        copy.start()

    for i in range(n_q):
        for h in range(heads):
            if fresh[i]:
                acc[i, h] = jnp.zeros(acc.shape[2:], jnp.float32)
                peaks[i, h] = jnp.full(peaks.shape[2:], FLOOR, jnp.float32)
            else:
                total, stat = states[i]
                acc[i, h, :, :HEAD_DIM] = total[:, pl.ds(h * HEAD_DIM, HEAD_DIM)]
                shape = (queries, HEAD_DIM)
                acc[i, h, :, HEAD_DIM:] = jnp.broadcast_to(
                    stat[:, heads + h : heads + h + 1], shape
                )
                peaks[i, h] = jnp.broadcast_to(stat[:, h : h + 1], shape)
    for copy in copies:
        copy.wait()

    ones = jnp.ones((2 * queries, HEAD_DIM), jnp.bfloat16)

    def step(i, f, times, window):
        factor = times.astype(jnp.float32)
        if window:
            outside, inside = log2_weight(times), log2_weight(times + 1)
            place = lax.broadcasted_iota(jnp.int32, (1, 2 * queries), 1)
            key_row = jnp.zeros((1, 2 * queries), jnp.int32)
            for r in range(1, 2 * rows):
                key_row = key_row + (place >= r * width).astype(jnp.int32)
            key_row = jnp.where(
                key_row < rows, key_row + band * rows, key_row - rows + (1 - band) * rows
            )
        for start in range(0, queries, BLOCK):
            part = pl.ds(start, BLOCK)
            if window:
                place = lax.broadcasted_iota(jnp.int32, (BLOCK, 1), 0) + start
                row = jnp.full((BLOCK, 1), -1000, jnp.int32)
                for r in range(rows):
                    valid = valid_refs[0][0, r]
                    if n_q > 1:
                        valid = jnp.where(i == 0, valid, valid_refs[1][0, r])
                    here = jnp.where(valid > 0, band * rows + r, -1000)
                    row = jnp.where((place >= r * width) & (place < (r + 1) * width), here, row)
                bias = jnp.where(jnp.abs(key_row - row) <= WINDOW, inside, outside)
            for h in range(heads):
                lanes = pl.ds(h * HEAD_DIM, HEAD_DIM)
                scores = (
                    lax.dot_general(
                        query_buf[i, part, lanes],
                        key_buf[f, :, lanes],
                        (((1,), (1,)), ((), ())),
                        preferred_element_type=jnp.float32,
                    )
                    * SCALE
                )
                if window:
                    scores = scores + bias
                old = peaks[i, h, part, :]
                peak = jnp.maximum(old, jnp.max(scores, axis=1, keepdims=True))
                terms = jnp.exp2(scores - peak[:, 0:1]).astype(jnp.bfloat16)
                value = jnp.concatenate([value_buf[f, :, lanes], ones], 1)
                mixed = jnp.dot(terms, value, preferred_element_type=jnp.float32)
                if not window:
                    mixed = mixed * factor
                fade = jnp.exp2(old - peak)
                acc[i, h, part, :] = (
                    acc[i, h, part, :] * jnp.concatenate([fade, fade], 1) + mixed
                )
                peaks[i, h, part, :] = peak

    def unit(u, carry):
        i, f = u // n_f, u % n_f
        times, window = plan(z, mem_ref[0], mem_ref[1], i, f)
        if windows:
            pl.when(window)(functools.partial(step, i, f, times, True))
            pl.when((times > 0) & jnp.logical_not(window))(
                functools.partial(step, i, f, times, False)
            )
        else:
            pl.when(times > 0)(functools.partial(step, i, f, times, False))
        return carry

    lax.fori_loop(0, n_q * n_f, unit, 0)

    for i in range(n_q):
        if finish[i]:
            for h in range(heads):
                outs[i][0][:, pl.ds(h * HEAD_DIM, HEAD_DIM)] = (
                    acc[i, h, :, :HEAD_DIM] / acc[i, h, :, HEAD_DIM:]
                ).astype(jnp.bfloat16)
        else:
            lane = lax.broadcasted_iota(jnp.int32, (1, HEAD_DIM), 1)
            stat = jnp.zeros((queries, HEAD_DIM), jnp.float32)
            for h in range(heads):
                outs[i][0][:, pl.ds(h * HEAD_DIM, HEAD_DIM)] = acc[i, h, :, :HEAD_DIM]
                stat = jnp.where(lane == h, peaks[i, h], stat)
                stat = jnp.where(lane == heads + h, acc[i, h, :, HEAD_DIM:], stat)
            outs[i][1][...] = stat


def attend(plan, windows, mem_index, valids, queries, frames, states, finish, width):
    n_q, n_f = len(queries), len(frames)
    tokens, channels = queries[0].shape
    heads = channels // HEAD_DIM
    scalars = pl.BlockSpec(memory_space=pltpu.SMEM)
    anywhere = pl.BlockSpec(memory_space=pltpu.HBM)
    whole = pl.BlockSpec(memory_space=pltpu.VMEM)
    fresh = tuple(s is None for s in states)
    operands = [mem_index, *valids, *queries]
    specs = [scalars] * (1 + n_q) + [anywhere] * n_q
    for frame in frames:
        operands += frame
        specs += [anywhere] * 4
    for state in states:
        if state is not None:
            operands += state
            specs += [whole] * 2
    shapes = []
    for done in finish:
        if done:
            shapes.append(jax.ShapeDtypeStruct((tokens, channels), jnp.bfloat16))
        else:
            shapes.append(jax.ShapeDtypeStruct((tokens, channels), jnp.float32))
            shapes.append(jax.ShapeDtypeStruct((tokens, HEAD_DIM), jnp.float32))
    outs = pl.pallas_call(
        functools.partial(
            attend_kernel, plan, n_q, n_f, fresh, tuple(finish), windows, width
        ),
        in_specs=specs,
        out_specs=[whole] * len(shapes),
        out_shape=shapes,
        scratch_shapes=[
            pltpu.VMEM((n_q, tokens, channels), jnp.bfloat16),
            pltpu.VMEM((n_f, 2 * tokens, channels), jnp.bfloat16),
            pltpu.VMEM((n_f, 2 * tokens, channels), jnp.bfloat16),
            pltpu.VMEM((n_q, heads, tokens, 2 * HEAD_DIM), jnp.float32),
            pltpu.VMEM((n_q, heads, tokens, HEAD_DIM), jnp.float32),
            pltpu.SemaphoreType.DMA((n_f + n_q, 2, 2)),
        ],
        compiler_params=pltpu.CompilerParams(vmem_limit_bytes=32 << 20),
        cost_estimate=pl.CostEstimate(
            flops=n_q * n_f * 8 * tokens * tokens * channels,
            transcendentals=n_q * n_f * 2 * tokens * tokens * heads,
            bytes_accessed=(n_f * 4 + n_q * 6) * tokens * channels * 2,
        ),
    )(*operands)
    outs = list(outs)
    return [outs.pop(0) if done else (outs.pop(0), outs.pop(0)) for done in finish]


def plan_four(sets, names, z, first, second, i, f):
    middle = (z == 1) | (z == 2)
    ids = (z, 3 - z, 3 * (z - 1), 6 - 3 * z)

    def pick(index, options):
        chosen = options[-1]
        for n in range(len(options) - 1):
            chosen = jnp.where(index == n, options[n], chosen)
        return chosen

    mine = pick(i, [(ids[0], ids[2])[s] for s in sets])
    frame = pick(f, [ids[n] for n in names])
    times = (
        (frame == mine).astype(jnp.int32)
        + (first == frame).astype(jnp.int32)
        + (second == frame).astype(jnp.int32)
    )
    return jnp.where(middle, times, 0), middle & (frame == mine - 1)


def plan_any(z, first, second, i, f):
    before = f == 1
    return jnp.where(before, 0, 1), before & (z > 0)


def with_other_half(key, value):
    return [key, value, swapped(key), swapped(value)]


def four_frames(queries, keys, values, valid_prev, mem_index):
    shape = queries.shape
    width = shape[2]
    tokens = shape[1] * width

    def flat(block):
        return block.reshape(tokens, shape[3])

    query, key, value = flat(queries), flat(keys), flat(values)
    inward = [(0, 1), (3, 2)]
    across = [(1, 2), (2, 1)]
    end_key, end_value = moved(key, inward), moved(value, inward)
    mid = with_other_half(moved(key, across), moved(value, across))
    own = with_other_half(key, value)
    end_key, end_value, late_query = lax.optimization_barrier((end_key, end_value, query))
    far_key, far_value = moved(end_key, across), moved(end_value, across)
    marks = jnp.broadcast_to(valid_prev[0][:, None], (shape[1], shape[3])).astype(jnp.bfloat16)
    marks = jnp.pad(marks, ((0, 16 - shape[1]), (0, 0)))
    end_query = moved(jnp.concatenate([late_query, marks], 0), inward)
    end_valid = end_query[tokens : tokens + shape[1], 0].astype(jnp.int32)[None]
    end_query = end_query[:tokens]
    end = with_other_half(end_key, end_value)
    (end_state,) = attend(
        functools.partial(plan_four, (1,), (0, 1, 2)),
        True,
        mem_index,
        [end_valid],
        [end_query],
        [own, mid, end],
        [None],
        [False],
        width,
    )
    far_key, far_value, end_state = lax.optimization_barrier((far_key, far_value, end_state))
    far = with_other_half(far_key, far_value)
    (end_out,) = attend(
        functools.partial(plan_four, (1,), (3,)),
        False,
        mem_index,
        [end_valid],
        [end_query],
        [far],
        [end_state],
        [True],
        width,
    )
    back = moved(end_out, [(1, 0), (2, 3)])
    (out,) = attend(
        functools.partial(plan_four, (0,), (0, 1, 2, 3)),
        True,
        mem_index,
        [valid_prev],
        [query],
        [own, mid, end, far],
        [None],
        [True],
        width,
    )
    z = lax.axis_index("frame")
    return jnp.where((z == 1) | (z == 2), out, back).reshape(shape)


def any_frames(queries, keys, values, valid_prev, mem_index):
    shape = queries.shape
    width = shape[2]
    tokens = shape[1] * width
    count = lax.axis_size("frame")
    z = lax.axis_index("frame")

    def flat(block):
        return block.reshape(tokens, shape[3])

    key, value = flat(keys), flat(values)
    onward = [(i, i + 1) for i in range(count - 1)]
    both = jnp.stack([key, value])
    masked = jnp.stack([jnp.where(z == mem_index[s], both, jnp.zeros_like(both)) for s in range(2)])
    memory = lax.psum(masked, "frame")
    frames = [
        with_other_half(key, value),
        with_other_half(moved(key, onward), moved(value, onward)),
        with_other_half(memory[0, 0], memory[0, 1]),
        with_other_half(memory[1, 0], memory[1, 1]),
    ]
    (out,) = attend(
        plan_any, True, mem_index, [valid_prev], [flat(queries)], frames, [None], [True], width
    )
    return out.reshape(shape)


def solution(mesh):
    spread = P(("groups", "frame"), "row", None, "head")
    body = four_frames if mesh.shape["frame"] == 4 else any_frames
    return jax.shard_map(
        body,
        mesh=mesh,
        in_specs=(spread, spread, spread, P(("groups", "frame"), "row"), P("groups")),
        out_specs=spread,
        check_vma=False,
    )
```

```python
import functools

import jax
import jax.numpy as jnp
from jax import lax
from jax.experimental import pallas as pl
from jax.experimental.pallas import tpu as pltpu
from jax.sharding import PartitionSpec as P

HEAD_DIM = 128
WINDOW = 2
SCALE = HEAD_DIM**-0.5 * 1.4426950408889634
FLOOR = -1e30
BLOCK = 128
LOG2_3 = 1.584962500721156
LONG = 20_000_000_000
SHORT = 1000


def moved(block, pairs):
    return lax.ppermute(block, "frame", pairs)


def swapped(block):
    return lax.ppermute(block, "row", [(0, 1), (1, 0)])


def log2_weight(count):
    return jnp.where(
        count < 1, -jnp.inf, jnp.where(count < 2, 0.0, jnp.where(count < 3, 1.0, LOG2_3))
    ).astype(jnp.float32)


def attend_kernel(plan, n_q, n_f, fresh, finish, windows, width, *refs):
    refs = list(refs)
    mem_ref = refs.pop(0)
    valid_refs = [refs.pop(0) for _ in range(n_q)]
    q_refs = [refs.pop(0) for _ in range(n_q)]
    frames = [[refs.pop(0) for _ in range(4)] for _ in range(n_f)]
    states = [None if fresh[i] else (refs.pop(0), refs.pop(0)) for i in range(n_q)]
    outs = [(refs.pop(0),) if finish[i] else (refs.pop(0), refs.pop(0)) for i in range(n_q)]
    query_buf, key_buf, value_buf, acc, peaks, sems = refs
    queries, channels = q_refs[0].shape
    heads = channels // HEAD_DIM
    rows = queries // width
    band = lax.axis_index("row")
    z = lax.axis_index("frame")

    copies = []
    for f in range(n_f):
        for half in range(2):
            for part, buf in enumerate((key_buf, value_buf)):
                copies.append(
                    pltpu.make_async_copy(
                        frames[f][2 * half + part].at[pl.ds(0, queries), :],
                        buf.at[f, pl.ds(half * queries, queries), :],
                        sems.at[f, half, part],
                    )
                )
    for i in range(n_q):
        copies.append(pltpu.make_async_copy(q_refs[i], query_buf.at[i], sems.at[n_f + i, 0, 0]))
    for copy in copies:
        copy.start()

    for i in range(n_q):
        for h in range(heads):
            if fresh[i]:
                acc[i, h] = jnp.zeros(acc.shape[2:], jnp.float32)
                peaks[i, h] = jnp.full(peaks.shape[2:], FLOOR, jnp.float32)
            else:
                total, stat = states[i]
                acc[i, h, :, :HEAD_DIM] = total[:, pl.ds(h * HEAD_DIM, HEAD_DIM)]
                shape = (queries, HEAD_DIM)
                acc[i, h, :, HEAD_DIM:] = jnp.broadcast_to(
                    stat[:, heads + h : heads + h + 1], shape
                )
                peaks[i, h] = jnp.broadcast_to(stat[:, h : h + 1], shape)
    for copy in copies:
        copy.wait()

    ones = jnp.ones((2 * queries, HEAD_DIM), jnp.bfloat16)

    def step(i, f, times, window):
        factor = times.astype(jnp.float32)
        if window:
            outside, inside = log2_weight(times), log2_weight(times + 1)
            place = lax.broadcasted_iota(jnp.int32, (1, 2 * queries), 1)
            key_row = jnp.zeros((1, 2 * queries), jnp.int32)
            for r in range(1, 2 * rows):
                key_row = key_row + (place >= r * width).astype(jnp.int32)
            key_row = jnp.where(
                key_row < rows, key_row + band * rows, key_row - rows + (1 - band) * rows
            )
        for start in range(0, queries, BLOCK):
            part = pl.ds(start, BLOCK)
            if window:
                place = lax.broadcasted_iota(jnp.int32, (BLOCK, 1), 0) + start
                row = jnp.full((BLOCK, 1), -1000, jnp.int32)
                for r in range(rows):
                    valid = valid_refs[0][0, r]
                    if n_q > 1:
                        valid = jnp.where(i == 0, valid, valid_refs[1][0, r])
                    here = jnp.where(valid > 0, band * rows + r, -1000)
                    row = jnp.where((place >= r * width) & (place < (r + 1) * width), here, row)
                bias = jnp.where(jnp.abs(key_row - row) <= WINDOW, inside, outside)
            for h in range(heads):
                lanes = pl.ds(h * HEAD_DIM, HEAD_DIM)
                scores = (
                    lax.dot_general(
                        query_buf[i, part, lanes],
                        key_buf[f, :, lanes],
                        (((1,), (1,)), ((), ())),
                        preferred_element_type=jnp.float32,
                    )
                    * SCALE
                )
                if window:
                    scores = scores + bias
                old = peaks[i, h, part, :]
                peak = jnp.maximum(old, jnp.max(scores, axis=1, keepdims=True))
                terms = jnp.exp2(scores - peak[:, 0:1]).astype(jnp.bfloat16)
                value = jnp.concatenate([value_buf[f, :, lanes], ones], 1)
                mixed = jnp.dot(terms, value, preferred_element_type=jnp.float32)
                if not window:
                    mixed = mixed * factor
                fade = jnp.exp2(old - peak)
                acc[i, h, part, :] = (
                    acc[i, h, part, :] * jnp.concatenate([fade, fade], 1) + mixed
                )
                peaks[i, h, part, :] = peak

    def unit(u, carry):
        i, f = u // n_f, u % n_f
        times, window = plan(z, mem_ref[0], mem_ref[1], i, f)
        if windows:
            pl.when(window)(functools.partial(step, i, f, times, True))
            pl.when((times > 0) & jnp.logical_not(window))(
                functools.partial(step, i, f, times, False)
            )
        else:
            pl.when(times > 0)(functools.partial(step, i, f, times, False))
        return carry

    lax.fori_loop(0, n_q * n_f, unit, 0)

    for i in range(n_q):
        if finish[i]:
            for h in range(heads):
                outs[i][0][:, pl.ds(h * HEAD_DIM, HEAD_DIM)] = (
                    acc[i, h, :, :HEAD_DIM] / acc[i, h, :, HEAD_DIM:]
                ).astype(jnp.bfloat16)
        else:
            lane = lax.broadcasted_iota(jnp.int32, (1, HEAD_DIM), 1)
            stat = jnp.zeros((queries, HEAD_DIM), jnp.float32)
            for h in range(heads):
                outs[i][0][:, pl.ds(h * HEAD_DIM, HEAD_DIM)] = acc[i, h, :, :HEAD_DIM]
                stat = jnp.where(lane == h, peaks[i, h], stat)
                stat = jnp.where(lane == heads + h, acc[i, h, :, HEAD_DIM:], stat)
            outs[i][1][...] = stat


def attend(plan, windows, mem_index, valids, queries, frames, states, finish, width, cost):
    n_q, n_f = len(queries), len(frames)
    tokens, channels = queries[0].shape
    heads = channels // HEAD_DIM
    scalars = pl.BlockSpec(memory_space=pltpu.SMEM)
    whole = pl.BlockSpec(memory_space=pltpu.VMEM)
    fresh = tuple(s is None for s in states)
    operands = [mem_index, *valids, *queries]
    specs = [scalars] * (1 + n_q) + [whole] * n_q
    for frame in frames:
        operands += frame
        specs += [whole] * 4
    for state in states:
        if state is not None:
            operands += state
            specs += [whole] * 2
    shapes = []
    for done in finish:
        if done:
            shapes.append(jax.ShapeDtypeStruct((tokens, channels), jnp.bfloat16))
        else:
            shapes.append(jax.ShapeDtypeStruct((tokens, channels), jnp.float32))
            shapes.append(jax.ShapeDtypeStruct((tokens, HEAD_DIM), jnp.float32))
    outs = pl.pallas_call(
        functools.partial(
            attend_kernel, plan, n_q, n_f, fresh, tuple(finish), windows, width
        ),
        in_specs=specs,
        out_specs=[whole] * len(shapes),
        out_shape=shapes,
        scratch_shapes=[
            pltpu.VMEM((n_q, tokens, channels), jnp.bfloat16),
            pltpu.VMEM((n_f, 2 * tokens, channels), jnp.bfloat16),
            pltpu.VMEM((n_f, 2 * tokens, channels), jnp.bfloat16),
            pltpu.VMEM((n_q, heads, tokens, 2 * HEAD_DIM), jnp.float32),
            pltpu.VMEM((n_q, heads, tokens, HEAD_DIM), jnp.float32),
            pltpu.SemaphoreType.DMA((n_f + n_q, 2, 2)),
        ],
        compiler_params=pltpu.CompilerParams(vmem_limit_bytes=16 << 20),
        cost_estimate=pl.CostEstimate(flops=cost, transcendentals=0, bytes_accessed=1000),
    )(*operands)
    outs = list(outs)
    return [outs.pop(0) if done else (outs.pop(0), outs.pop(0)) for done in finish]


def plan_four(sets, names, z, first, second, i, f):
    middle = (z == 1) | (z == 2)
    ids = (z, 3 - z, 3 * (z - 1), 6 - 3 * z)

    def pick(index, options):
        chosen = options[-1]
        for n in range(len(options) - 1):
            chosen = jnp.where(index == n, options[n], chosen)
        return chosen

    mine = pick(i, [(ids[0], ids[2])[s] for s in sets])
    frame = pick(f, [ids[n] for n in names])
    times = (
        (frame == mine).astype(jnp.int32)
        + (first == frame).astype(jnp.int32)
        + (second == frame).astype(jnp.int32)
    )
    return jnp.where(middle, times, 0), middle & (frame == mine - 1)


def plan_any(z, first, second, i, f):
    before = f == 1
    return jnp.where(before, 0, 1), before & (z > 0)


def with_other_half(key, value):
    return [key, value, swapped(key), swapped(value)]


def four_frames(queries, keys, values, valid_prev, mem_index):
    shape = queries.shape
    width = shape[2]
    tokens = shape[1] * width

    def flat(block):
        return block.reshape(tokens, shape[3])

    query, key, value = flat(queries), flat(keys), flat(values)
    inward = [(0, 1), (3, 2)]
    across = [(1, 2), (2, 1)]
    marks = jnp.broadcast_to(valid_prev[0][:, None], (shape[1], shape[3])).astype(jnp.bfloat16)
    marks = jnp.pad(marks, ((0, 16 - shape[1]), (0, 0)))
    end_key = moved(key, inward)
    end_value = moved(jnp.concatenate([value, marks], 0), inward)
    mid_key, mid_value = moved(key, across), moved(value, across)
    end_query = moved(query, inward)
    own = with_other_half(key, value)
    far_key, far_value = moved(end_key, across), moved(end_value, across)
    end_valid = end_value[tokens : tokens + shape[1], 0].astype(jnp.int32)[None]
    (state,) = attend(
        functools.partial(plan_four, (0,), (0,)),
        False,
        mem_index,
        [valid_prev],
        [query],
        [own],
        [None],
        [False],
        width,
        LONG,
    )
    mid_key, mid_value, end_key, end_value, state = lax.optimization_barrier(
        (mid_key, mid_value, end_key, end_value, state)
    )
    mid = with_other_half(mid_key, mid_value)
    end = with_other_half(end_key, end_value)
    (end_state,) = attend(
        functools.partial(plan_four, (1,), (0, 1, 2)),
        True,
        mem_index,
        [end_valid],
        [end_query],
        [own, mid, end],
        [None],
        [False],
        width,
        SHORT,
    )
    far_key, far_value, end_state = lax.optimization_barrier((far_key, far_value, end_state))
    far = with_other_half(far_key, far_value)
    (end_out,) = attend(
        functools.partial(plan_four, (1,), (3,)),
        False,
        mem_index,
        [end_valid],
        [end_query],
        [far],
        [end_state],
        [True],
        width,
        SHORT,
    )
    back = moved(end_out, [(1, 0), (2, 3)])
    (out,) = attend(
        functools.partial(plan_four, (0,), (1, 2, 3)),
        True,
        mem_index,
        [valid_prev],
        [query],
        [mid, end, far],
        [state],
        [True],
        width,
        LONG,
    )
    z = lax.axis_index("frame")
    return jnp.where((z == 1) | (z == 2), out, back).reshape(shape)


def any_frames(queries, keys, values, valid_prev, mem_index):
    shape = queries.shape
    width = shape[2]
    tokens = shape[1] * width
    count = lax.axis_size("frame")
    z = lax.axis_index("frame")

    def flat(block):
        return block.reshape(tokens, shape[3])

    key, value = flat(keys), flat(values)
    onward = [(i, i + 1) for i in range(count - 1)]
    both = jnp.stack([key, value])
    masked = jnp.stack([jnp.where(z == mem_index[s], both, jnp.zeros_like(both)) for s in range(2)])
    memory = lax.psum(masked, "frame")
    frames = [
        with_other_half(key, value),
        with_other_half(moved(key, onward), moved(value, onward)),
        with_other_half(memory[0, 0], memory[0, 1]),
        with_other_half(memory[1, 0], memory[1, 1]),
    ]
    (out,) = attend(
        plan_any, True, mem_index, [valid_prev], [flat(queries)], frames, [None], [True], width, LONG
    )
    return out.reshape(shape)


def solution(mesh):
    spread = P(("groups", "frame"), "row", None, "head")
    body = four_frames if mesh.shape["frame"] == 4 else any_frames
    return jax.shard_map(
        body,
        mesh=mesh,
        in_specs=(spread, spread, spread, P(("groups", "frame"), "row"), P("groups")),
        out_specs=spread,
        check_vma=False,
    )
```

```python
import functools

import jax
import jax.numpy as jnp
from jax import lax
from jax.experimental import pallas as pl
from jax.experimental.pallas import tpu as pltpu
from jax.sharding import PartitionSpec as P

HEAD_DIM = 128
WINDOW = 2
SCALE = HEAD_DIM**-0.5 * 1.4426950408889634
FLOOR = -1e30
BLOCK = 128
LOG2_3 = 1.584962500721156
LONG = 20_000_000_000
SHORT = 1000


def moved(block, pairs):
    return lax.ppermute(block, "frame", pairs)


def swapped(block):
    return lax.ppermute(block, "row", [(0, 1), (1, 0)])


def log2_weight(count):
    return jnp.where(
        count < 1, -jnp.inf, jnp.where(count < 2, 0.0, jnp.where(count < 3, 1.0, LOG2_3))
    ).astype(jnp.float32)


def attend_kernel(plan, windows, n_f, fresh, finish, width, *refs):
    refs = list(refs)
    mem_ref, valid_ref, q_ref = refs[:3]
    frames = [refs[3 + 2 * f : 5 + 2 * f] for f in range(n_f)]
    acc, peaks = refs[-2:]
    queries, channels = q_ref.shape
    heads = channels // HEAD_DIM
    rows = queries // width
    band = lax.axis_index("row")
    z = lax.axis_index("frame")

    if fresh:
        acc[...] = jnp.zeros_like(acc)
        peaks[...] = jnp.full(peaks.shape, FLOOR, jnp.float32)
    ones = jnp.ones((2 * queries, HEAD_DIM), jnp.bfloat16)

    def step(f, times, window):
        factor = times.astype(jnp.float32)
        if window:
            outside, inside = log2_weight(times), log2_weight(times + 1)
            place = lax.broadcasted_iota(jnp.int32, (1, 2 * queries), 1)
            key_row = jnp.zeros((1, 2 * queries), jnp.int32)
            for r in range(1, 2 * rows):
                key_row = key_row + (place >= r * width).astype(jnp.int32)
            key_row = jnp.where(
                key_row < rows, key_row + band * rows, key_row - rows + (1 - band) * rows
            )
        for start in range(0, queries, BLOCK):
            part = pl.ds(start, BLOCK)
            if window:
                place = lax.broadcasted_iota(jnp.int32, (BLOCK, 1), 0) + start
                row = jnp.full((BLOCK, 1), -1000, jnp.int32)
                for r in range(rows):
                    here = jnp.where(valid_ref[0, r] > 0, band * rows + r, -1000)
                    row = jnp.where((place >= r * width) & (place < (r + 1) * width), here, row)
                bias = jnp.where(jnp.abs(key_row - row) <= WINDOW, inside, outside)
            for h in range(heads):
                lanes = pl.ds(h * HEAD_DIM, HEAD_DIM)
                key, value = [
                    jnp.concatenate([half[pl.ds(n * queries, queries), lanes] for half in frames[f]], 0)
                    for n in range(2)
                ]
                scores = (
                    lax.dot_general(
                        q_ref[part, lanes],
                        key,
                        (((1,), (1,)), ((), ())),
                        preferred_element_type=jnp.float32,
                    )
                    * SCALE
                )
                if window:
                    scores = scores + bias
                old = peaks[h, part, :]
                peak = jnp.maximum(old, jnp.max(scores, axis=1, keepdims=True))
                terms = jnp.exp2(scores - peak[:, 0:1]).astype(jnp.bfloat16)
                mixed = jnp.dot(
                    terms,
                    jnp.concatenate([value, ones], 1),
                    preferred_element_type=jnp.float32,
                )
                if not window:
                    mixed = mixed * factor
                fade = jnp.exp2(old - peak)
                acc[h, part, :] = acc[h, part, :] * jnp.concatenate([fade, fade], 1) + mixed
                peaks[h, part, :] = peak

    for f in range(n_f):
        times, window = plan(z, mem_ref[0], mem_ref[1], f)
        if windows[f]:
            pl.when(window)(functools.partial(step, f, times, True))
            pl.when((times > 0) & jnp.logical_not(window))(
                functools.partial(step, f, times, False)
            )
        else:
            pl.when(times > 0)(functools.partial(step, f, times, False))

    if finish:
        out = refs[-3]
        for h in range(heads):
            out[:, pl.ds(h * HEAD_DIM, HEAD_DIM)] = (
                acc[h, :, :HEAD_DIM] / acc[h, :, HEAD_DIM:]
            ).astype(jnp.bfloat16)


def attend(plan, windows, mem_index, valid, query, frames, state, finish, width, cost):
    tokens, channels = query.shape
    heads = channels // HEAD_DIM
    scalars = pl.BlockSpec(memory_space=pltpu.SMEM)
    whole = pl.BlockSpec(memory_space=pltpu.VMEM)
    operands = [mem_index, valid, query]
    for frame in frames:
        operands += frame
    shapes = [
        jax.ShapeDtypeStruct((heads, tokens, 2 * HEAD_DIM), jnp.float32),
        jax.ShapeDtypeStruct((heads, tokens, HEAD_DIM), jnp.float32),
    ]
    if finish:
        shapes = [jax.ShapeDtypeStruct((tokens, channels), jnp.bfloat16)] + shapes
    aliases = {}
    if state is not None:
        aliases = {len(operands) + n: len(shapes) - 2 + n for n in range(2)}
        operands += state
    outs = pl.pallas_call(
        functools.partial(
            attend_kernel, plan, windows, len(frames), state is None, finish, width
        ),
        in_specs=[scalars] * 2 + [whole] * (len(operands) - 2),
        out_specs=[whole] * len(shapes),
        out_shape=shapes,
        input_output_aliases=aliases,
        compiler_params=pltpu.CompilerParams(vmem_limit_bytes=16 << 20),
        cost_estimate=pl.CostEstimate(flops=cost, transcendentals=0, bytes_accessed=1000),
    )(*operands)
    return outs[0] if finish else list(outs)


def plan_four(query_set, names, z, first, second, f):
    middle = (z == 1) | (z == 2)
    ids = (z, 3 - z, 3 * (z - 1), 6 - 3 * z)
    mine, frame = ids[2 * query_set], ids[names[f]]
    times = (
        (frame == mine).astype(jnp.int32)
        + (first == frame).astype(jnp.int32)
        + (second == frame).astype(jnp.int32)
    )
    return jnp.where(middle, times, 0), middle & (frame == mine - 1)


def plan_any(z, first, second, f):
    return jnp.int32(0 if f == 1 else 1), z > 0


def four_frames(queries, keys, values, valid_prev, mem_index):
    shape = queries.shape
    width = shape[2]
    tokens = shape[1] * width

    def flat(block):
        return block.reshape(tokens, shape[3])

    query = flat(queries)
    inward = [(0, 1), (3, 2)]
    across = [(1, 2), (2, 1)]
    marks = jnp.broadcast_to(valid_prev[0][:, None], (shape[1], shape[3])).astype(jnp.bfloat16)
    marks = jnp.pad(marks, ((0, 16 - shape[1]), (0, 0)))
    own = jnp.concatenate([flat(keys), flat(values), marks], 0)
    end = moved(own, inward)
    mid = moved(own, across)
    end_query = moved(query, inward)
    own = [own, swapped(own)]
    far = moved(end, across)
    end_valid = end[2 * tokens : 2 * tokens + shape[1], 0].astype(jnp.int32)[None]
    state = attend(
        functools.partial(plan_four, 0, (0,)),
        (False,),
        mem_index,
        valid_prev,
        query,
        [own],
        None,
        False,
        width,
        LONG,
    )
    mid = [mid, swapped(mid)]
    end = [end, swapped(end)]
    end_state = attend(
        functools.partial(plan_four, 1, (0, 1, 2)),
        (True, False, False),
        mem_index,
        end_valid,
        end_query,
        [own, mid, end],
        None,
        False,
        width,
        SHORT,
    )
    far, end_state = lax.optimization_barrier((far, end_state))
    far = [far, swapped(far)]
    end_out = attend(
        functools.partial(plan_four, 1, (3,)),
        (False,),
        mem_index,
        end_valid,
        end_query,
        [far],
        end_state,
        True,
        width,
        SHORT,
    )
    back = moved(end_out, [(1, 0), (2, 3)])
    out = attend(
        functools.partial(plan_four, 0, (1, 2, 3)),
        (True, True, False),
        mem_index,
        valid_prev,
        query,
        [mid, end, far],
        state,
        True,
        width,
        LONG,
    )
    z = lax.axis_index("frame")
    return jnp.where((z == 1) | (z == 2), out, back).reshape(shape)


def any_frames(queries, keys, values, valid_prev, mem_index):
    shape = queries.shape
    width = shape[2]
    tokens = shape[1] * width
    count = lax.axis_size("frame")
    z = lax.axis_index("frame")

    def flat(block):
        return block.reshape(tokens, shape[3])

    own = jnp.concatenate([flat(keys), flat(values)], 0)
    before = moved(own, [(i, i + 1) for i in range(count - 1)])
    masked = jnp.stack([jnp.where(z == mem_index[s], own, jnp.zeros_like(own)) for s in range(2)])
    memory = lax.psum(masked, "frame")
    out = attend(
        plan_any,
        (False, True, False, False),
        mem_index,
        valid_prev,
        flat(queries),
        [[kv, swapped(kv)] for kv in (own, before, memory[0], memory[1])],
        None,
        True,
        width,
        LONG,
    )
    return out.reshape(shape)


def solution(mesh):
    spread = P(("groups", "frame"), "row", None, "head")
    body = four_frames if mesh.shape["frame"] == 4 else any_frames
    return jax.shard_map(
        body,
        mesh=mesh,
        in_specs=(spread, spread, spread, P(("groups", "frame"), "row"), P("groups")),
        out_specs=spread,
        check_vma=False,
    )
```

```python
import functools

import jax
import jax.numpy as jnp
from jax import lax
from jax.experimental import pallas as pl
from jax.experimental.pallas import tpu as pltpu
from jax.sharding import PartitionSpec as P

HEAD_DIM = 128
WINDOW = 2
SCALE = HEAD_DIM**-0.5 * 1.4426950408889634
FLOOR = -1e30
BLOCK = 128
LOG2_3 = 1.584962500721156
LONG = 20_000_000_000
SHORT = 1000


def moved(block, pairs):
    return lax.ppermute(block, "frame", pairs)


def swapped(block):
    return lax.ppermute(block, "row", [(0, 1), (1, 0)])


def log2_weight(count):
    return jnp.where(
        count < 1, -jnp.inf, jnp.where(count < 2, 0.0, jnp.where(count < 3, 1.0, LOG2_3))
    ).astype(jnp.float32)


def attend_kernel(plan, windows, marked, n_f, fresh, finish, width, *refs):
    refs = list(refs)
    mem_ref, valid_ref, q_ref = refs[:3]
    frames = [refs[3 + 2 * f : 5 + 2 * f] for f in range(n_f)]
    acc, peaks = refs[-2:]
    queries, channels = q_ref.shape
    heads = channels // HEAD_DIM
    rows = queries // width
    band = lax.axis_index("row")
    z = lax.axis_index("frame")

    if fresh:
        acc[...] = jnp.zeros_like(acc)
        peaks[...] = jnp.full(peaks.shape, FLOOR, jnp.float32)
    ones = jnp.ones((2 * queries, HEAD_DIM), jnp.bfloat16)

    def step(f, times, window):
        factor = times.astype(jnp.float32)
        if window:
            outside, inside = log2_weight(times), log2_weight(times + 1)
            if marked is not None:
                marks = frames[marked][0][pl.ds(2 * queries, 16), 0:HEAD_DIM].astype(jnp.float32)
            place = lax.broadcasted_iota(jnp.int32, (1, 2 * queries), 1)
            key_row = jnp.zeros((1, 2 * queries), jnp.int32)
            for r in range(1, 2 * rows):
                key_row = key_row + (place >= r * width).astype(jnp.int32)
            key_row = jnp.where(
                key_row < rows, key_row + band * rows, key_row - rows + (1 - band) * rows
            )
        for start in range(0, queries, BLOCK):
            part = pl.ds(start, BLOCK)
            if window:
                place = lax.broadcasted_iota(jnp.int32, (BLOCK, 1), 0) + start
                row = jnp.full((BLOCK, 1), -1000, jnp.int32)
                for r in range(rows):
                    here = (place >= r * width) & (place < (r + 1) * width)
                    if marked is None:
                        here = here & (valid_ref[0, r] > 0)
                    else:
                        here = here & (marks[r : r + 1, 0:1] > 0.0)
                    row = jnp.where(here, band * rows + r, row)
                bias = jnp.where(jnp.abs(key_row - row) <= WINDOW, inside, outside)
            for h in range(heads):
                lanes = pl.ds(h * HEAD_DIM, HEAD_DIM)
                key, value = [
                    jnp.concatenate([half[pl.ds(n * queries, queries), lanes] for half in frames[f]], 0)
                    for n in range(2)
                ]
                scores = (
                    lax.dot_general(
                        q_ref[part, lanes],
                        key,
                        (((1,), (1,)), ((), ())),
                        preferred_element_type=jnp.float32,
                    )
                    * SCALE
                )
                if window:
                    scores = scores + bias
                old = peaks[h, part, :]
                peak = jnp.maximum(old, jnp.max(scores, axis=1, keepdims=True))
                terms = jnp.exp2(scores - peak[:, 0:1]).astype(jnp.bfloat16)
                mixed = jnp.dot(
                    terms,
                    jnp.concatenate([value, ones], 1),
                    preferred_element_type=jnp.float32,
                )
                if not window:
                    mixed = mixed * factor
                fade = jnp.exp2(old - peak)
                acc[h, part, :] = acc[h, part, :] * jnp.concatenate([fade, fade], 1) + mixed
                peaks[h, part, :] = peak

    for f in range(n_f):
        times, window = plan(z, mem_ref[0], mem_ref[1], f)
        if windows[f]:
            pl.when(window)(functools.partial(step, f, times, True))
            pl.when((times > 0) & jnp.logical_not(window))(
                functools.partial(step, f, times, False)
            )
        else:
            pl.when(times > 0)(functools.partial(step, f, times, False))

    if finish:
        out = refs[-3]
        for h in range(heads):
            out[:, pl.ds(h * HEAD_DIM, HEAD_DIM)] = (
                acc[h, :, :HEAD_DIM] / acc[h, :, HEAD_DIM:]
            ).astype(jnp.bfloat16)


def attend(plan, windows, mem_index, valid, query, frames, state, finish, width, cost, marked=None):
    tokens, channels = query.shape
    heads = channels // HEAD_DIM
    scalars = pl.BlockSpec(memory_space=pltpu.SMEM)
    whole = pl.BlockSpec(memory_space=pltpu.VMEM)
    operands = [mem_index, valid, query]
    for frame in frames:
        operands += frame
    shapes = [
        jax.ShapeDtypeStruct((heads, tokens, 2 * HEAD_DIM), jnp.float32),
        jax.ShapeDtypeStruct((heads, tokens, HEAD_DIM), jnp.float32),
    ]
    if finish:
        shapes = [jax.ShapeDtypeStruct((tokens, channels), jnp.bfloat16)] + shapes
    aliases = {}
    if state is not None:
        aliases = {len(operands) + n: len(shapes) - 2 + n for n in range(2)}
        operands += state
    outs = pl.pallas_call(
        functools.partial(
            attend_kernel,
            plan,
            windows,
            marked,
            len(frames),
            state is None,
            finish,
            width,
        ),
        in_specs=[scalars] * 2 + [whole] * (len(operands) - 2),
        out_specs=[whole] * len(shapes),
        out_shape=shapes,
        input_output_aliases=aliases,
        compiler_params=pltpu.CompilerParams(vmem_limit_bytes=16 << 20),
        cost_estimate=pl.CostEstimate(flops=cost, transcendentals=0, bytes_accessed=1000),
    )(*operands)
    return outs[0] if finish else list(outs)


def stack_kernel(valid_ref, key_ref, value_ref, out_ref, sems):
    tokens = key_ref.shape[0]
    copies = [
        pltpu.make_async_copy(ref, out_ref.at[pl.ds(n * tokens, tokens), :], sems.at[n])
        for n, ref in enumerate((key_ref, value_ref))
    ]
    for copy in copies:
        copy.start()
    place = lax.broadcasted_iota(jnp.int32, (16, out_ref.shape[1]), 0)
    marks = jnp.zeros(place.shape, jnp.float32)
    for r in range(valid_ref.shape[1]):
        marks = jnp.where((place == r) & (valid_ref[0, r] > 0), 1.0, marks)
    out_ref[pl.ds(2 * tokens, 16), :] = marks.astype(jnp.bfloat16)
    for copy in copies:
        copy.wait()


def stacked(valid, key, value):
    anywhere = pl.BlockSpec(memory_space=pl.ANY)
    return pl.pallas_call(
        stack_kernel,
        in_specs=[pl.BlockSpec(memory_space=pltpu.SMEM), anywhere, anywhere],
        out_specs=pl.BlockSpec(memory_space=pltpu.VMEM),
        out_shape=jax.ShapeDtypeStruct((2 * key.shape[0] + 16, key.shape[1]), jnp.bfloat16),
        scratch_shapes=[pltpu.SemaphoreType.DMA((2,))],
        cost_estimate=pl.CostEstimate(flops=SHORT, transcendentals=0, bytes_accessed=1000),
    )(valid, key, value)


def plan_four(query_set, names, z, first, second, f):
    middle = (z == 1) | (z == 2)
    ids = (z, 3 - z, 3 * (z - 1), 6 - 3 * z)
    mine, frame = ids[2 * query_set], ids[names[f]]
    times = (
        (frame == mine).astype(jnp.int32)
        + (first == frame).astype(jnp.int32)
        + (second == frame).astype(jnp.int32)
    )
    return jnp.where(middle, times, 0), middle & (frame == mine - 1)


def plan_any(z, first, second, f):
    return jnp.int32(0 if f == 1 else 1), z > 0


def four_frames(queries, keys, values, valid_prev, mem_index):
    shape = queries.shape
    width = shape[2]
    tokens = shape[1] * width

    def flat(block):
        return block.reshape(tokens, shape[3])

    query = flat(queries)
    inward = [(0, 1), (3, 2)]
    across = [(1, 2), (2, 1)]
    own = stacked(valid_prev, flat(keys), flat(values))
    end = moved(own, inward)
    mid = moved(own, across)
    end_query = moved(query, inward)
    own = [own, swapped(own)]
    far = moved(end, across)
    state = attend(
        functools.partial(plan_four, 0, (0,)),
        (False,),
        mem_index,
        valid_prev,
        query,
        [own],
        None,
        False,
        width,
        LONG,
    )
    mid, late_end, state = lax.optimization_barrier((mid, end, state))
    mid = [mid, swapped(mid)]
    end = [late_end, swapped(late_end)]
    end_state = attend(
        functools.partial(plan_four, 1, (0, 1, 2)),
        (True, False, False),
        mem_index,
        valid_prev,
        end_query,
        [own, mid, end],
        None,
        False,
        width,
        SHORT,
        marked=2,
    )
    far, end_state = lax.optimization_barrier((far, end_state))
    far = [far, swapped(far)]
    end_out = attend(
        functools.partial(plan_four, 1, (3,)),
        (False,),
        mem_index,
        valid_prev,
        end_query,
        [far],
        end_state,
        True,
        width,
        SHORT,
    )
    back = moved(end_out, [(1, 0), (2, 3)])
    out = attend(
        functools.partial(plan_four, 0, (1, 2, 3)),
        (True, True, False),
        mem_index,
        valid_prev,
        query,
        [mid, end, far],
        state,
        True,
        width,
        LONG,
    )
    z = lax.axis_index("frame")
    return jnp.where((z == 1) | (z == 2), out, back).reshape(shape)


def any_frames(queries, keys, values, valid_prev, mem_index):
    shape = queries.shape
    width = shape[2]
    tokens = shape[1] * width
    count = lax.axis_size("frame")
    z = lax.axis_index("frame")

    def flat(block):
        return block.reshape(tokens, shape[3])

    own = jnp.concatenate([flat(keys), flat(values)], 0)
    before = moved(own, [(i, i + 1) for i in range(count - 1)])
    masked = jnp.stack([jnp.where(z == mem_index[s], own, jnp.zeros_like(own)) for s in range(2)])
    memory = lax.psum(masked, "frame")
    out = attend(
        plan_any,
        (False, True, False, False),
        mem_index,
        valid_prev,
        flat(queries),
        [[kv, swapped(kv)] for kv in (own, before, memory[0], memory[1])],
        None,
        True,
        width,
        LONG,
    )
    return out.reshape(shape)


def solution(mesh):
    spread = P(("groups", "frame"), "row", None, "head")
    body = four_frames if mesh.shape["frame"] == 4 else any_frames
    return jax.shard_map(
        body,
        mesh=mesh,
        in_specs=(spread, spread, spread, P(("groups", "frame"), "row"), P("groups")),
        out_specs=spread,
        check_vma=False,
    )
```

```python
import functools

import jax
import jax.numpy as jnp
from jax import lax
from jax.experimental import pallas as pl
from jax.experimental.pallas import tpu as pltpu
from jax.sharding import PartitionSpec as P

HEAD_DIM = 128
WINDOW = 2
SCALE = HEAD_DIM**-0.5 * 1.4426950408889634
FLOOR = -1e30
BLOCK = 128
LOG2_3 = 1.584962500721156
LONG = 20_000_000_000
SHORT = 1000


def moved(block, pairs):
    return lax.ppermute(block, "frame", pairs)


def swapped(block):
    return lax.ppermute(block, "row", [(0, 1), (1, 0)])


def log2_weight(count):
    return jnp.where(
        count < 1, -jnp.inf, jnp.where(count < 2, 0.0, jnp.where(count < 3, 1.0, LOG2_3))
    ).astype(jnp.float32)


def attend_kernel(plan, windows, marked, n_f, fresh, finish, width, *refs):
    refs = list(refs)
    mem_ref, valid_ref, q_ref = refs[:3]
    frames = [refs[3 + 2 * f : 5 + 2 * f] for f in range(n_f)]
    acc, peaks = refs[-2:]
    queries, channels = frames[0][0].shape
    queries //= 2
    heads = channels // HEAD_DIM
    rows = queries // width
    band = lax.axis_index("row")
    z = lax.axis_index("frame")

    if fresh:
        acc[...] = jnp.zeros_like(acc)
        peaks[...] = jnp.full(peaks.shape, FLOOR, jnp.float32)
    ones = jnp.ones((2 * queries, HEAD_DIM), jnp.bfloat16)

    def step(f, times, window):
        factor = times.astype(jnp.float32)
        if window:
            outside, inside = log2_weight(times), log2_weight(times + 1)
            if marked:
                marks = q_ref[pl.ds(queries, 16), 0:HEAD_DIM].astype(jnp.float32)
            place = lax.broadcasted_iota(jnp.int32, (1, 2 * queries), 1)
            key_row = jnp.zeros((1, 2 * queries), jnp.int32)
            for r in range(1, 2 * rows):
                key_row = key_row + (place >= r * width).astype(jnp.int32)
            key_row = jnp.where(
                key_row < rows, key_row + band * rows, key_row - rows + (1 - band) * rows
            )
        for start in range(0, queries, BLOCK):
            part = pl.ds(start, BLOCK)
            if window:
                place = lax.broadcasted_iota(jnp.int32, (BLOCK, 1), 0) + start
                row = jnp.full((BLOCK, 1), -1000, jnp.int32)
                for r in range(rows):
                    here = (place >= r * width) & (place < (r + 1) * width)
                    if marked:
                        here = here & (marks[r : r + 1, 0:1] > 0.0)
                    else:
                        here = here & (valid_ref[0, r] > 0)
                    row = jnp.where(here, band * rows + r, row)
                bias = jnp.where(jnp.abs(key_row - row) <= WINDOW, inside, outside)
            for h in range(heads):
                lanes = pl.ds(h * HEAD_DIM, HEAD_DIM)
                key, value = [
                    jnp.concatenate([half[pl.ds(n * queries, queries), lanes] for half in frames[f]], 0)
                    for n in range(2)
                ]
                scores = (
                    lax.dot_general(
                        q_ref[part, lanes],
                        key,
                        (((1,), (1,)), ((), ())),
                        preferred_element_type=jnp.float32,
                    )
                    * SCALE
                )
                if window:
                    scores = scores + bias
                old = peaks[h, part, :]
                peak = jnp.maximum(old, jnp.max(scores, axis=1, keepdims=True))
                terms = jnp.exp2(scores - peak[:, 0:1]).astype(jnp.bfloat16)
                mixed = jnp.dot(
                    terms,
                    jnp.concatenate([value, ones], 1),
                    preferred_element_type=jnp.float32,
                )
                if not window:
                    mixed = mixed * factor
                fade = jnp.exp2(old - peak)
                acc[h, part, :] = acc[h, part, :] * jnp.concatenate([fade, fade], 1) + mixed
                peaks[h, part, :] = peak

    for f in range(n_f):
        times, window = plan(z, mem_ref[0], mem_ref[1], f)
        if windows[f]:
            pl.when(window)(functools.partial(step, f, times, True))
            pl.when((times > 0) & jnp.logical_not(window))(
                functools.partial(step, f, times, False)
            )
        else:
            pl.when(times > 0)(functools.partial(step, f, times, False))

    if finish:
        out = refs[-3]
        for h in range(heads):
            out[:, pl.ds(h * HEAD_DIM, HEAD_DIM)] = (
                acc[h, :, :HEAD_DIM] / acc[h, :, HEAD_DIM:]
            ).astype(jnp.bfloat16)


def attend(
    plan, windows, mem_index, valid, query, frames, state, finish, width, cost, marked=False
):
    tokens, channels = frames[0][0].shape
    tokens //= 2
    heads = channels // HEAD_DIM
    scalars = pl.BlockSpec(memory_space=pltpu.SMEM)
    whole = pl.BlockSpec(memory_space=pltpu.VMEM)
    operands = [mem_index, valid, query]
    for frame in frames:
        operands += frame
    shapes = [
        jax.ShapeDtypeStruct((heads, tokens, 2 * HEAD_DIM), jnp.float32),
        jax.ShapeDtypeStruct((heads, tokens, HEAD_DIM), jnp.float32),
    ]
    if finish:
        shapes = [jax.ShapeDtypeStruct((tokens, channels), jnp.bfloat16)] + shapes
    aliases, scratch = {}, []
    if finish and state is None:
        scratch = [pltpu.VMEM(s.shape, s.dtype) for s in shapes[1:]]
        shapes = shapes[:1]
    if state is not None:
        aliases = {len(operands) + n: len(shapes) - 2 + n for n in range(2)}
        operands += state
    outs = pl.pallas_call(
        functools.partial(
            attend_kernel,
            plan,
            windows,
            marked,
            len(frames),
            state is None,
            finish,
            width,
        ),
        in_specs=[scalars] * 2 + [whole] * (len(operands) - 2),
        out_specs=[whole] * len(shapes),
        out_shape=shapes,
        input_output_aliases=aliases,
        scratch_shapes=scratch,
        compiler_params=pltpu.CompilerParams(vmem_limit_bytes=16 << 20),
        cost_estimate=pl.CostEstimate(flops=cost, transcendentals=0, bytes_accessed=1000),
    )(*operands)
    return outs[0] if finish else list(outs)


def marker(mem_index):
    def kernel(mem_ref, out_ref):
        for n in range(mem_ref.shape[0]):
            out_ref[n] = mem_ref[n]

    scalars = pl.BlockSpec(memory_space=pltpu.SMEM)
    return pl.pallas_call(
        kernel,
        in_specs=[scalars],
        out_specs=scalars,
        out_shape=jax.ShapeDtypeStruct(mem_index.shape, jnp.int32),
        cost_estimate=pl.CostEstimate(flops=LONG, transcendentals=0, bytes_accessed=1000),
    )(mem_index)


def plan_four(query_set, names, z, first, second, f):
    middle = (z == 1) | (z == 2)
    ids = (z, 3 - z, 3 * (z - 1), 6 - 3 * z)
    mine, frame = ids[2 * query_set], ids[names[f]]
    times = (
        (frame == mine).astype(jnp.int32)
        + (first == frame).astype(jnp.int32)
        + (second == frame).astype(jnp.int32)
    )
    return jnp.where(middle, times, 0), middle & (frame == mine - 1)


def plan_any(z, first, second, f):
    return jnp.int32(0 if f == 1 else 1), z > 0


def four_frames(queries, keys, values, valid_prev, mem_index):
    shape = queries.shape
    width = shape[2]
    tokens = shape[1] * width

    def flat(block):
        return block.reshape(tokens, shape[3])

    query = flat(queries)
    inward = [(0, 1), (3, 2)]
    across = [(1, 2), (2, 1)]
    own = jnp.concatenate([flat(keys), flat(values)], 0)
    end = moved(own, inward)
    mid = moved(own, across)
    own = [own, swapped(own)]
    far = moved(end, across)
    marks = jnp.broadcast_to(valid_prev[0][:, None], (shape[1], shape[3])).astype(jnp.bfloat16)
    marks = jnp.pad(marks, ((0, 16 - shape[1]), (0, 0)))
    end_query = moved(jnp.concatenate([query, marks], 0), inward)
    mid = [mid, swapped(mid)]
    end = [end, swapped(end)]
    end_state = attend(
        functools.partial(plan_four, 1, (0, 1, 2)),
        (True, False, False),
        marker(mem_index),
        valid_prev,
        end_query,
        [own, mid, end],
        None,
        False,
        width,
        SHORT,
        marked=True,
    )
    far, end_state = lax.optimization_barrier((far, end_state))
    far = [far, swapped(far)]
    end_out = attend(
        functools.partial(plan_four, 1, (3,)),
        (False,),
        mem_index,
        valid_prev,
        end_query,
        [far],
        end_state,
        True,
        width,
        SHORT,
    )
    back = moved(end_out, [(1, 0), (2, 3)])
    out = attend(
        functools.partial(plan_four, 0, (0, 1, 2, 3)),
        (False, True, True, False),
        mem_index,
        valid_prev,
        query,
        [own, mid, end, far],
        None,
        True,
        width,
        LONG,
    )
    z = lax.axis_index("frame")
    return jnp.where((z == 1) | (z == 2), out, back).reshape(shape)


def any_frames(queries, keys, values, valid_prev, mem_index):
    shape = queries.shape
    width = shape[2]
    tokens = shape[1] * width
    count = lax.axis_size("frame")
    z = lax.axis_index("frame")

    def flat(block):
        return block.reshape(tokens, shape[3])

    own = jnp.concatenate([flat(keys), flat(values)], 0)
    before = moved(own, [(i, i + 1) for i in range(count - 1)])
    masked = jnp.stack([jnp.where(z == mem_index[s], own, jnp.zeros_like(own)) for s in range(2)])
    memory = lax.psum(masked, "frame")
    out = attend(
        plan_any,
        (False, True, False, False),
        mem_index,
        valid_prev,
        flat(queries),
        [[kv, swapped(kv)] for kv in (own, before, memory[0], memory[1])],
        None,
        True,
        width,
        LONG,
    )
    return out.reshape(shape)


def solution(mesh):
    spread = P(("groups", "frame"), "row", None, "head")
    body = four_frames if mesh.shape["frame"] == 4 else any_frames
    return jax.shard_map(
        body,
        mesh=mesh,
        in_specs=(spread, spread, spread, P(("groups", "frame"), "row"), P("groups")),
        out_specs=spread,
        check_vma=False,
    )
```

```python
import functools

import jax
import jax.numpy as jnp
from jax import lax
from jax.experimental import pallas as pl
from jax.experimental.pallas import tpu as pltpu
from jax.sharding import PartitionSpec as P

HEAD_DIM = 128
WINDOW = 2
SCALE = HEAD_DIM**-0.5 * 1.4426950408889634
FLOOR = -1e30
BLOCK = 128
LOG2_3 = 1.584962500721156
LONG = 20_000_000_000
SHORT = 1000


def moved(block, pairs):
    return lax.ppermute(block, "frame", pairs)


def swapped(block):
    return lax.ppermute(block, "row", [(0, 1), (1, 0)])


def log2_weight(count):
    return jnp.where(
        count < 1, -jnp.inf, jnp.where(count < 2, 0.0, jnp.where(count < 3, 1.0, LOG2_3))
    ).astype(jnp.float32)


def attend_kernel(plan, windows, marked, n_f, fresh, finish, width, *refs):
    refs = list(refs)
    mem_ref, valid_ref, q_ref = refs[:3]
    frames = [refs[3 + 2 * f : 5 + 2 * f] for f in range(n_f)]
    acc, peaks = refs[-2:]
    lane = lax.broadcasted_iota(jnp.int32, (1, HEAD_DIM), 1)
    queries, channels = frames[0][0].shape
    queries //= 2
    heads = channels // HEAD_DIM
    rows = queries // width
    band = lax.axis_index("row")
    z = lax.axis_index("frame")

    if fresh:
        acc[...] = jnp.zeros_like(acc)
        peaks[...] = jnp.full(peaks.shape, FLOOR, jnp.float32)
    else:
        total, stat = refs[3 + 2 * n_f : 5 + 2 * n_f]
        for h in range(heads):
            acc[h, :, :HEAD_DIM] = total[:, pl.ds(h * HEAD_DIM, HEAD_DIM)]
            shape = (queries, HEAD_DIM)
            peaks[h] = jnp.broadcast_to(stat[:, h : h + 1], shape)
            acc[h, :, HEAD_DIM:] = jnp.broadcast_to(stat[:, heads + h : heads + h + 1], shape)
    ones = jnp.ones((2 * queries, HEAD_DIM), jnp.bfloat16)

    def step(f, times, window):
        factor = times.astype(jnp.float32)
        if window:
            outside, inside = log2_weight(times), log2_weight(times + 1)
            if marked:
                marks = q_ref[pl.ds(queries, 16), 0:HEAD_DIM].astype(jnp.float32)
            place = lax.broadcasted_iota(jnp.int32, (1, 2 * queries), 1)
            key_row = jnp.zeros((1, 2 * queries), jnp.int32)
            for r in range(1, 2 * rows):
                key_row = key_row + (place >= r * width).astype(jnp.int32)
            key_row = jnp.where(
                key_row < rows, key_row + band * rows, key_row - rows + (1 - band) * rows
            )
        for start in range(0, queries, BLOCK):
            part = pl.ds(start, BLOCK)
            if window:
                place = lax.broadcasted_iota(jnp.int32, (BLOCK, 1), 0) + start
                row = jnp.full((BLOCK, 1), -1000, jnp.int32)
                for r in range(rows):
                    here = (place >= r * width) & (place < (r + 1) * width)
                    if marked:
                        here = here & (marks[r : r + 1, 0:1] > 0.0)
                    else:
                        here = here & (valid_ref[0, r] > 0)
                    row = jnp.where(here, band * rows + r, row)
                bias = jnp.where(jnp.abs(key_row - row) <= WINDOW, inside, outside)
            for h in range(heads):
                lanes = pl.ds(h * HEAD_DIM, HEAD_DIM)
                key, value = [
                    jnp.concatenate([half[pl.ds(n * queries, queries), lanes] for half in frames[f]], 0)
                    for n in range(2)
                ]
                scores = (
                    lax.dot_general(
                        q_ref[part, lanes],
                        key,
                        (((1,), (1,)), ((), ())),
                        preferred_element_type=jnp.float32,
                    )
                    * SCALE
                )
                if window:
                    scores = scores + bias
                old = peaks[h, part, :]
                peak = jnp.maximum(old, jnp.max(scores, axis=1, keepdims=True))
                terms = jnp.exp2(scores - peak[:, 0:1]).astype(jnp.bfloat16)
                mixed = jnp.dot(
                    terms,
                    jnp.concatenate([value, ones], 1),
                    preferred_element_type=jnp.float32,
                )
                if not window:
                    mixed = mixed * factor
                fade = jnp.exp2(old - peak)
                acc[h, part, :] = acc[h, part, :] * jnp.concatenate([fade, fade], 1) + mixed
                peaks[h, part, :] = peak

    for f in range(n_f):
        times, window = plan(z, mem_ref[0], mem_ref[1], f)
        if windows[f]:
            pl.when(window)(functools.partial(step, f, times, True))
            pl.when((times > 0) & jnp.logical_not(window))(
                functools.partial(step, f, times, False)
            )
        else:
            pl.when(times > 0)(functools.partial(step, f, times, False))

    if finish:
        out = refs[-3]
        for h in range(heads):
            out[:, pl.ds(h * HEAD_DIM, HEAD_DIM)] = (
                acc[h, :, :HEAD_DIM] / acc[h, :, HEAD_DIM:]
            ).astype(jnp.bfloat16)
    else:
        total, stat = refs[-4:-2]
        packed = jnp.zeros((queries, HEAD_DIM), jnp.float32)
        for h in range(heads):
            total[:, pl.ds(h * HEAD_DIM, HEAD_DIM)] = acc[h, :, :HEAD_DIM]
            packed = jnp.where(lane == h, peaks[h], packed)
            packed = jnp.where(lane == heads + h, acc[h, :, HEAD_DIM:], packed)
        stat[...] = packed


def attend(
    plan, windows, mem_index, valid, query, frames, state, finish, width, cost, marked=False
):
    tokens, channels = frames[0][0].shape
    tokens //= 2
    heads = channels // HEAD_DIM
    scalars = pl.BlockSpec(memory_space=pltpu.SMEM)
    whole = pl.BlockSpec(memory_space=pltpu.VMEM)
    operands = [mem_index, valid, query]
    for frame in frames:
        operands += frame
    if state is not None:
        operands += state
    shapes = [jax.ShapeDtypeStruct((tokens, channels), jnp.bfloat16)]
    if not finish:
        shapes = [
            jax.ShapeDtypeStruct((tokens, channels), jnp.float32),
            jax.ShapeDtypeStruct((tokens, HEAD_DIM), jnp.float32),
        ]
    outs = pl.pallas_call(
        functools.partial(
            attend_kernel,
            plan,
            windows,
            marked,
            len(frames),
            state is None,
            finish,
            width,
        ),
        in_specs=[scalars] * 2 + [whole] * (len(operands) - 2),
        out_specs=[whole] * len(shapes),
        out_shape=shapes,
        scratch_shapes=[
            pltpu.VMEM((heads, tokens, 2 * HEAD_DIM), jnp.float32),
            pltpu.VMEM((heads, tokens, HEAD_DIM), jnp.float32),
        ],
        compiler_params=pltpu.CompilerParams(vmem_limit_bytes=16 << 20),
        cost_estimate=pl.CostEstimate(flops=cost, transcendentals=0, bytes_accessed=1000),
    )(*operands)
    return outs[0] if finish else list(outs)


def marker(mem_index):
    def kernel(mem_ref, out_ref):
        for n in range(mem_ref.shape[0]):
            out_ref[n] = mem_ref[n]

    scalars = pl.BlockSpec(memory_space=pltpu.SMEM)
    return pl.pallas_call(
        kernel,
        in_specs=[scalars],
        out_specs=scalars,
        out_shape=jax.ShapeDtypeStruct(mem_index.shape, jnp.int32),
        cost_estimate=pl.CostEstimate(flops=LONG, transcendentals=0, bytes_accessed=1000),
    )(mem_index)


def plan_four(query_set, names, z, first, second, f):
    middle = (z == 1) | (z == 2)
    ids = (z, 3 - z, 3 * (z - 1), 6 - 3 * z)
    mine, frame = ids[2 * query_set], ids[names[f]]
    times = (
        (frame == mine).astype(jnp.int32)
        + (first == frame).astype(jnp.int32)
        + (second == frame).astype(jnp.int32)
    )
    return jnp.where(middle, times, 0), middle & (frame == mine - 1)


def plan_any(z, first, second, f):
    return jnp.int32(0 if f == 1 else 1), z > 0


def four_frames(queries, keys, values, valid_prev, mem_index):
    shape = queries.shape
    width = shape[2]
    tokens = shape[1] * width

    def flat(block):
        return block.reshape(tokens, shape[3])

    query = flat(queries)
    inward = [(0, 1), (3, 2)]
    across = [(1, 2), (2, 1)]
    own = jnp.concatenate([flat(keys), flat(values)], 0)
    end = moved(own, inward)
    mid = moved(own, across)
    own = [own, swapped(own)]
    far = moved(end, across)
    marks = jnp.broadcast_to(valid_prev[0][:, None], (shape[1], shape[3])).astype(jnp.bfloat16)
    marks = jnp.pad(marks, ((0, 16 - shape[1]), (0, 0)))
    end_query = moved(jnp.concatenate([query, marks], 0), inward)
    mid = [mid, swapped(mid)]
    end = [end, swapped(end)]
    end_state = attend(
        functools.partial(plan_four, 1, (0, 1, 2)),
        (True, False, False),
        marker(mem_index),
        valid_prev,
        end_query,
        [own, mid, end],
        None,
        False,
        width,
        SHORT,
        marked=True,
    )
    far, end_state = lax.optimization_barrier((far, end_state))
    far = [far, swapped(far)]
    end_out = attend(
        functools.partial(plan_four, 1, (3,)),
        (False,),
        mem_index,
        valid_prev,
        end_query,
        [far],
        end_state,
        True,
        width,
        SHORT,
    )
    back = moved(end_out, [(1, 0), (2, 3)])
    out = attend(
        functools.partial(plan_four, 0, (0, 1, 2, 3)),
        (False, True, True, False),
        mem_index,
        valid_prev,
        query,
        [own, mid, end, far],
        None,
        True,
        width,
        LONG,
    )
    z = lax.axis_index("frame")
    return jnp.where((z == 1) | (z == 2), out, back).reshape(shape)


def any_frames(queries, keys, values, valid_prev, mem_index):
    shape = queries.shape
    width = shape[2]
    tokens = shape[1] * width
    count = lax.axis_size("frame")
    z = lax.axis_index("frame")

    def flat(block):
        return block.reshape(tokens, shape[3])

    own = jnp.concatenate([flat(keys), flat(values)], 0)
    before = moved(own, [(i, i + 1) for i in range(count - 1)])
    masked = jnp.stack([jnp.where(z == mem_index[s], own, jnp.zeros_like(own)) for s in range(2)])
    memory = lax.psum(masked, "frame")
    out = attend(
        plan_any,
        (False, True, False, False),
        mem_index,
        valid_prev,
        flat(queries),
        [[kv, swapped(kv)] for kv in (own, before, memory[0], memory[1])],
        None,
        True,
        width,
        LONG,
    )
    return out.reshape(shape)


def solution(mesh):
    spread = P(("groups", "frame"), "row", None, "head")
    body = four_frames if mesh.shape["frame"] == 4 else any_frames
    return jax.shard_map(
        body,
        mesh=mesh,
        in_specs=(spread, spread, spread, P(("groups", "frame"), "row"), P("groups")),
        out_specs=spread,
        check_vma=False,
    )
```

```python
import functools

import jax
import jax.numpy as jnp
from jax import lax
from jax.experimental import pallas as pl
from jax.experimental.pallas import tpu as pltpu
from jax.sharding import PartitionSpec as P

HEAD_DIM = 128
WINDOW = 2
SCALE = HEAD_DIM**-0.5 * 1.4426950408889634
FLOOR = -1e30
BLOCK = 128
LOG2_3 = 1.584962500721156
LONG = 20_000_000_000
SHORT = 1000


def moved(block, pairs):
    return lax.ppermute(block, "frame", pairs)


def swapped(block):
    return lax.ppermute(block, "row", [(0, 1), (1, 0)])


def log2_weight(count):
    return jnp.where(
        count < 1, -jnp.inf, jnp.where(count < 2, 0.0, jnp.where(count < 3, 1.0, LOG2_3))
    ).astype(jnp.float32)


def attend_kernel(plan, windows, marked, n_f, fresh, finish, width, *refs):
    refs = list(refs)
    mem_ref, valid_ref, q_ref = refs[:3]
    frames = [refs[3 + 2 * f : 5 + 2 * f] for f in range(n_f)]
    n_in = 3 + 2 * n_f + (0 if fresh else 2)
    acc, peaks = refs[n_in + 2 - finish : n_in + 4 - finish]
    lane = lax.broadcasted_iota(jnp.int32, (1, HEAD_DIM), 1)
    queries, channels = frames[0][0].shape
    queries //= 2
    heads = channels // HEAD_DIM
    rows = queries // width
    band = lax.axis_index("row")
    z = lax.axis_index("frame")

    if fresh:
        acc[...] = jnp.zeros_like(acc)
        peaks[...] = jnp.full(peaks.shape, FLOOR, jnp.float32)
    else:
        total, stat, sems = refs[-3:]
        copies = [
            pltpu.make_async_copy(refs[n_in - 2 + n], buf, sems.at[n])
            for n, buf in enumerate((total, stat))
        ]
        for copy in copies:
            copy.start()
        for copy in copies:
            copy.wait()
        for h in range(heads):
            acc[h, :, :HEAD_DIM] = total[:, pl.ds(h * HEAD_DIM, HEAD_DIM)]
            shape = (queries, HEAD_DIM)
            peaks[h] = jnp.broadcast_to(stat[:, h : h + 1], shape)
            acc[h, :, HEAD_DIM:] = jnp.broadcast_to(stat[:, heads + h : heads + h + 1], shape)
    ones = jnp.ones((2 * queries, HEAD_DIM), jnp.bfloat16)

    def step(f, times, window):
        factor = times.astype(jnp.float32)
        if window:
            outside, inside = log2_weight(times), log2_weight(times + 1)
            if marked:
                marks = q_ref[pl.ds(queries, 16), 0:HEAD_DIM].astype(jnp.float32)
            place = lax.broadcasted_iota(jnp.int32, (1, 2 * queries), 1)
            key_row = jnp.zeros((1, 2 * queries), jnp.int32)
            for r in range(1, 2 * rows):
                key_row = key_row + (place >= r * width).astype(jnp.int32)
            key_row = jnp.where(
                key_row < rows, key_row + band * rows, key_row - rows + (1 - band) * rows
            )
        for start in range(0, queries, BLOCK):
            part = pl.ds(start, BLOCK)
            if window:
                place = lax.broadcasted_iota(jnp.int32, (BLOCK, 1), 0) + start
                row = jnp.full((BLOCK, 1), -1000, jnp.int32)
                for r in range(rows):
                    here = (place >= r * width) & (place < (r + 1) * width)
                    if marked:
                        here = here & (marks[r : r + 1, 0:1] > 0.0)
                    else:
                        here = here & (valid_ref[0, r] > 0)
                    row = jnp.where(here, band * rows + r, row)
                bias = jnp.where(jnp.abs(key_row - row) <= WINDOW, inside, outside)
            for h in range(heads):
                lanes = pl.ds(h * HEAD_DIM, HEAD_DIM)
                key, value = [
                    jnp.concatenate([half[pl.ds(n * queries, queries), lanes] for half in frames[f]], 0)
                    for n in range(2)
                ]
                scores = (
                    lax.dot_general(
                        q_ref[part, lanes],
                        key,
                        (((1,), (1,)), ((), ())),
                        preferred_element_type=jnp.float32,
                    )
                    * SCALE
                )
                if window:
                    scores = scores + bias
                old = peaks[h, part, :]
                peak = jnp.maximum(old, jnp.max(scores, axis=1, keepdims=True))
                terms = jnp.exp2(scores - peak[:, 0:1]).astype(jnp.bfloat16)
                mixed = jnp.dot(
                    terms,
                    jnp.concatenate([value, ones], 1),
                    preferred_element_type=jnp.float32,
                )
                if not window:
                    mixed = mixed * factor
                fade = jnp.exp2(old - peak)
                acc[h, part, :] = acc[h, part, :] * jnp.concatenate([fade, fade], 1) + mixed
                peaks[h, part, :] = peak

    for f in range(n_f):
        times, window = plan(z, mem_ref[0], mem_ref[1], f)
        if windows[f]:
            pl.when(window)(functools.partial(step, f, times, True))
            pl.when((times > 0) & jnp.logical_not(window))(
                functools.partial(step, f, times, False)
            )
        else:
            pl.when(times > 0)(functools.partial(step, f, times, False))

    if finish:
        out = refs[n_in]
        for h in range(heads):
            out[:, pl.ds(h * HEAD_DIM, HEAD_DIM)] = (
                acc[h, :, :HEAD_DIM] / acc[h, :, HEAD_DIM:]
            ).astype(jnp.bfloat16)
    else:
        total, stat = refs[n_in : n_in + 2]
        packed = jnp.zeros((queries, HEAD_DIM), jnp.float32)
        for h in range(heads):
            total[:, pl.ds(h * HEAD_DIM, HEAD_DIM)] = acc[h, :, :HEAD_DIM]
            packed = jnp.where(lane == h, peaks[h], packed)
            packed = jnp.where(lane == heads + h, acc[h, :, HEAD_DIM:], packed)
        stat[...] = packed


def attend(
    plan, windows, mem_index, valid, query, frames, state, finish, width, cost, marked=False
):
    tokens, channels = frames[0][0].shape
    tokens //= 2
    heads = channels // HEAD_DIM
    scalars = pl.BlockSpec(memory_space=pltpu.SMEM)
    whole = pl.BlockSpec(memory_space=pltpu.VMEM)
    operands = [mem_index, valid, query]
    for frame in frames:
        operands += frame
    if state is not None:
        operands += [pltpu.with_memory_space_constraint(s, pltpu.HBM) for s in state]
    shapes = [jax.ShapeDtypeStruct((tokens, channels), jnp.bfloat16)]
    if not finish:
        shapes = [
            jax.ShapeDtypeStruct((tokens, channels), jnp.float32),
            jax.ShapeDtypeStruct((tokens, HEAD_DIM), jnp.float32),
        ]
    scratch = [
        pltpu.VMEM((heads, tokens, 2 * HEAD_DIM), jnp.float32),
        pltpu.VMEM((heads, tokens, HEAD_DIM), jnp.float32),
    ]
    specs = [scalars] * 2 + [whole] * (1 + 2 * len(frames))
    if state is not None:
        specs += [pl.BlockSpec(memory_space=pltpu.HBM)] * 2
        scratch += [pltpu.VMEM(s.shape, s.dtype) for s in state]
        scratch.append(pltpu.SemaphoreType.DMA((2,)))
    outs = pl.pallas_call(
        functools.partial(
            attend_kernel,
            plan,
            windows,
            marked,
            len(frames),
            state is None,
            finish,
            width,
        ),
        in_specs=specs,
        out_specs=[whole] * len(shapes),
        out_shape=shapes,
        scratch_shapes=scratch,
        compiler_params=pltpu.CompilerParams(vmem_limit_bytes=16 << 20),
        cost_estimate=pl.CostEstimate(flops=cost, transcendentals=0, bytes_accessed=1000),
    )(*operands)
    return outs[0] if finish else list(outs)


def marker(mem_index):
    def kernel(mem_ref, out_ref):
        for n in range(mem_ref.shape[0]):
            out_ref[n] = mem_ref[n]

    scalars = pl.BlockSpec(memory_space=pltpu.SMEM)
    return pl.pallas_call(
        kernel,
        in_specs=[scalars],
        out_specs=scalars,
        out_shape=jax.ShapeDtypeStruct(mem_index.shape, jnp.int32),
        cost_estimate=pl.CostEstimate(flops=LONG, transcendentals=0, bytes_accessed=1000),
    )(mem_index)


def plan_four(query_set, names, z, first, second, f):
    middle = (z == 1) | (z == 2)
    ids = (z, 3 - z, 3 * (z - 1), 6 - 3 * z)
    mine, frame = ids[2 * query_set], ids[names[f]]
    times = (
        (frame == mine).astype(jnp.int32)
        + (first == frame).astype(jnp.int32)
        + (second == frame).astype(jnp.int32)
    )
    return jnp.where(middle, times, 0), middle & (frame == mine - 1)


def plan_any(z, first, second, f):
    return jnp.int32(0 if f == 1 else 1), z > 0


def four_frames(queries, keys, values, valid_prev, mem_index):
    shape = queries.shape
    width = shape[2]
    tokens = shape[1] * width

    def flat(block):
        return block.reshape(tokens, shape[3])

    query = flat(queries)
    inward = [(0, 1), (3, 2)]
    across = [(1, 2), (2, 1)]
    own = jnp.concatenate([flat(keys), flat(values)], 0)
    end = moved(own, inward)
    mid = moved(own, across)
    own = [own, swapped(own)]
    far = moved(end, across)
    marks = jnp.broadcast_to(valid_prev[0][:, None], (shape[1], shape[3])).astype(jnp.bfloat16)
    marks = jnp.pad(marks, ((0, 16 - shape[1]), (0, 0)))
    end_query = moved(jnp.concatenate([query, marks], 0), inward)
    mid = [mid, swapped(mid)]
    end = [end, swapped(end)]
    memory = marker(mem_index)
    end_state = attend(
        functools.partial(plan_four, 1, (0, 1, 2)),
        (True, False, False),
        memory,
        valid_prev,
        end_query,
        [own, mid, end],
        None,
        False,
        width,
        SHORT,
        marked=True,
    )
    far, end_state = lax.optimization_barrier((far, end_state))
    far = [far, swapped(far)]
    end_out = attend(
        functools.partial(plan_four, 1, (3,)),
        (False,),
        memory,
        valid_prev,
        end_query,
        [far],
        end_state,
        True,
        width,
        SHORT,
    )
    back = moved(end_out, [(1, 0), (2, 3)])
    out = attend(
        functools.partial(plan_four, 0, (0, 1, 2, 3)),
        (False, True, True, False),
        memory,
        valid_prev,
        query,
        [own, mid, end, far],
        None,
        True,
        width,
        LONG,
    )
    z = lax.axis_index("frame")
    return jnp.where((z == 1) | (z == 2), out, back).reshape(shape)


def any_frames(queries, keys, values, valid_prev, mem_index):
    shape = queries.shape
    width = shape[2]
    tokens = shape[1] * width
    count = lax.axis_size("frame")
    z = lax.axis_index("frame")

    def flat(block):
        return block.reshape(tokens, shape[3])

    own = jnp.concatenate([flat(keys), flat(values)], 0)
    before = moved(own, [(i, i + 1) for i in range(count - 1)])
    masked = jnp.stack([jnp.where(z == mem_index[s], own, jnp.zeros_like(own)) for s in range(2)])
    memory = lax.psum(masked, "frame")
    out = attend(
        plan_any,
        (False, True, False, False),
        mem_index,
        valid_prev,
        flat(queries),
        [[kv, swapped(kv)] for kv in (own, before, memory[0], memory[1])],
        None,
        True,
        width,
        LONG,
    )
    return out.reshape(shape)


def solution(mesh):
    spread = P(("groups", "frame"), "row", None, "head")
    body = four_frames if mesh.shape["frame"] == 4 else any_frames
    return jax.shard_map(
        body,
        mesh=mesh,
        in_specs=(spread, spread, spread, P(("groups", "frame"), "row"), P("groups")),
        out_specs=spread,
        check_vma=False,
    )
```

```python
import functools

import jax
import jax.numpy as jnp
from jax import lax
from jax.experimental import pallas as pl
from jax.experimental.pallas import tpu as pltpu
from jax.sharding import PartitionSpec as P

HEAD_DIM = 128
WINDOW = 2
SCALE = HEAD_DIM**-0.5 * 1.4426950408889634
FLOOR = -1e30
BLOCK = 128
LOG2_3 = 1.584962500721156
LONG = 20_000_000_000
SHORT = 1000


def moved(block, pairs):
    return lax.ppermute(block, "frame", pairs)


def swapped(block):
    return lax.ppermute(block, "row", [(0, 1), (1, 0)])


def log2_weight(count):
    return jnp.where(
        count < 1, -jnp.inf, jnp.where(count < 2, 0.0, jnp.where(count < 3, 1.0, LOG2_3))
    ).astype(jnp.float32)


def attend_kernel(plan, windows, marked, first_head, n_f, fresh, finish, width, *refs):
    refs = list(refs)
    mem_ref, valid_ref, q_ref = refs[:3]
    frames = [refs[3 + 2 * f : 5 + 2 * f] for f in range(n_f)]
    n_in = 3 + 2 * n_f + (0 if fresh else 2)
    acc, peaks = refs[n_in + 2 : n_in + 4]
    lane = lax.broadcasted_iota(jnp.int32, (1, HEAD_DIM), 1)
    queries, channels = frames[0][0].shape
    queries //= 2
    heads = channels // HEAD_DIM
    rows = queries // width
    band = lax.axis_index("row")
    z = lax.axis_index("frame")

    if fresh:
        acc[...] = jnp.zeros_like(acc)
        peaks[...] = jnp.full(peaks.shape, FLOOR, jnp.float32)
    else:
        total, stat, sems = refs[-3:]
        copies = [
            pltpu.make_async_copy(refs[n_in - 2 + n], buf, sems.at[n])
            for n, buf in enumerate((total, stat))
        ]
        for copy in copies:
            copy.start()
        for copy in copies:
            copy.wait()
        for h in range(heads):
            acc[h, :, :HEAD_DIM] = total[:, pl.ds(h * HEAD_DIM, HEAD_DIM)]
            shape = (queries, HEAD_DIM)
            peaks[h] = jnp.broadcast_to(stat[:, h : h + 1], shape)
            acc[h, :, HEAD_DIM:] = jnp.broadcast_to(stat[:, heads + h : heads + h + 1], shape)
    ones = jnp.ones((2 * queries, HEAD_DIM), jnp.bfloat16)

    def step(f, times, window):
        factor = times.astype(jnp.float32)
        if window:
            outside, inside = log2_weight(times), log2_weight(times + 1)
            if marked:
                marks = q_ref[pl.ds(queries, 16), 0:HEAD_DIM].astype(jnp.float32)
            place = lax.broadcasted_iota(jnp.int32, (1, 2 * queries), 1)
            key_row = jnp.zeros((1, 2 * queries), jnp.int32)
            for r in range(1, 2 * rows):
                key_row = key_row + (place >= r * width).astype(jnp.int32)
            key_row = jnp.where(
                key_row < rows, key_row + band * rows, key_row - rows + (1 - band) * rows
            )
        for start in range(0, queries, BLOCK):
            part = pl.ds(start, BLOCK)
            if window:
                place = lax.broadcasted_iota(jnp.int32, (BLOCK, 1), 0) + start
                row = jnp.full((BLOCK, 1), -1000, jnp.int32)
                for r in range(rows):
                    here = (place >= r * width) & (place < (r + 1) * width)
                    if marked:
                        here = here & (marks[r : r + 1, 0:1] > 0.0)
                    else:
                        here = here & (valid_ref[0, r] > 0)
                    row = jnp.where(here, band * rows + r, row)
                bias = jnp.where(jnp.abs(key_row - row) <= WINDOW, inside, outside)
            for h in range(heads):
                lanes = pl.ds(h * HEAD_DIM, HEAD_DIM)
                key, value = [
                    jnp.concatenate([half[pl.ds(n * queries, queries), lanes] for half in frames[f]], 0)
                    for n in range(2)
                ]
                scores = (
                    lax.dot_general(
                        q_ref[part, pl.ds((first_head + h) * HEAD_DIM, HEAD_DIM)],
                        key,
                        (((1,), (1,)), ((), ())),
                        preferred_element_type=jnp.float32,
                    )
                    * SCALE
                )
                if window:
                    scores = scores + bias
                old = peaks[h, part, :]
                peak = jnp.maximum(old, jnp.max(scores, axis=1, keepdims=True))
                terms = jnp.exp2(scores - peak[:, 0:1]).astype(jnp.bfloat16)
                mixed = jnp.dot(
                    terms,
                    jnp.concatenate([value, ones], 1),
                    preferred_element_type=jnp.float32,
                )
                if not window:
                    mixed = mixed * factor
                fade = jnp.exp2(old - peak)
                acc[h, part, :] = acc[h, part, :] * jnp.concatenate([fade, fade], 1) + mixed
                peaks[h, part, :] = peak

    for f in range(n_f):
        times, window = plan(z, mem_ref[0], mem_ref[1], f)
        if windows[f]:
            pl.when(window)(functools.partial(step, f, times, True))
            pl.when((times > 0) & jnp.logical_not(window))(
                functools.partial(step, f, times, False)
            )
        else:
            pl.when(times > 0)(functools.partial(step, f, times, False))

    if finish:
        out = refs[n_in]
        for n in range(mem_ref.shape[0]):
            refs[n_in + 1][n] = mem_ref[n]
        for h in range(heads):
            out[:, pl.ds(h * HEAD_DIM, HEAD_DIM)] = (
                acc[h, :, :HEAD_DIM] / acc[h, :, HEAD_DIM:]
            ).astype(jnp.bfloat16)
    else:
        total, stat = refs[n_in : n_in + 2]
        packed = jnp.zeros((queries, HEAD_DIM), jnp.float32)
        for h in range(heads):
            total[:, pl.ds(h * HEAD_DIM, HEAD_DIM)] = acc[h, :, :HEAD_DIM]
            packed = jnp.where(lane == h, peaks[h], packed)
            packed = jnp.where(lane == heads + h, acc[h, :, HEAD_DIM:], packed)
        stat[...] = packed


def attend(
    plan,
    windows,
    mem_index,
    valid,
    query,
    first_head,
    frames,
    state,
    finish,
    width,
    cost,
    marked=False,
):
    tokens, channels = frames[0][0].shape
    tokens //= 2
    heads = channels // HEAD_DIM
    scalars = pl.BlockSpec(memory_space=pltpu.SMEM)
    whole = pl.BlockSpec(memory_space=pltpu.VMEM)
    operands = [mem_index, valid, query]
    for frame in frames:
        operands += frame
    if state is not None:
        operands += [pltpu.with_memory_space_constraint(s, pltpu.HBM) for s in state]
    shapes = [
        jax.ShapeDtypeStruct((tokens, channels), jnp.bfloat16),
        jax.ShapeDtypeStruct(mem_index.shape, jnp.int32),
    ]
    if not finish:
        shapes = [
            jax.ShapeDtypeStruct((tokens, channels), jnp.float32),
            jax.ShapeDtypeStruct((tokens, HEAD_DIM), jnp.float32),
        ]
    scratch = [
        pltpu.VMEM((heads, tokens, 2 * HEAD_DIM), jnp.float32),
        pltpu.VMEM((heads, tokens, HEAD_DIM), jnp.float32),
    ]
    specs = [scalars] * 2 + [whole] * (1 + 2 * len(frames))
    if state is not None:
        specs += [pl.BlockSpec(memory_space=pltpu.HBM)] * 2
        scratch += [pltpu.VMEM(s.shape, s.dtype) for s in state]
        scratch.append(pltpu.SemaphoreType.DMA((2,)))
    outs = pl.pallas_call(
        functools.partial(
            attend_kernel,
            plan,
            windows,
            marked,
            first_head,
            len(frames),
            state is None,
            finish,
            width,
        ),
        in_specs=specs,
        out_specs=[whole, scalars if finish else whole],
        out_shape=shapes,
        scratch_shapes=scratch,
        compiler_params=pltpu.CompilerParams(vmem_limit_bytes=16 << 20),
        cost_estimate=pl.CostEstimate(flops=cost, transcendentals=0, bytes_accessed=1000),
    )(*operands)
    return list(outs)


def marker(mem_index):
    def kernel(mem_ref, out_ref):
        for n in range(mem_ref.shape[0]):
            out_ref[n] = mem_ref[n]

    scalars = pl.BlockSpec(memory_space=pltpu.SMEM)
    return pl.pallas_call(
        kernel,
        in_specs=[scalars],
        out_specs=scalars,
        out_shape=jax.ShapeDtypeStruct(mem_index.shape, jnp.int32),
        cost_estimate=pl.CostEstimate(flops=LONG, transcendentals=0, bytes_accessed=1000),
    )(mem_index)


def plan_four(query_set, names, z, first, second, f):
    middle = (z == 1) | (z == 2)
    ids = (z, 3 - z, 3 * (z - 1), 6 - 3 * z)
    mine, frame = ids[2 * query_set], ids[names[f]]
    times = (
        (frame == mine).astype(jnp.int32)
        + (first == frame).astype(jnp.int32)
        + (second == frame).astype(jnp.int32)
    )
    return jnp.where(middle, times, 0), middle & (frame == mine - 1)


def plan_any(z, first, second, f):
    return jnp.int32(0 if f == 1 else 1), z > 0


def four_frames(queries, keys, values, valid_prev, mem_index):
    shape = queries.shape
    width = shape[2]
    tokens = shape[1] * width

    def flat(block):
        return block.reshape(tokens, shape[3])

    query, key, value = flat(queries), flat(keys), flat(values)
    inward = [(0, 1), (3, 2)]
    across = [(1, 2), (2, 1)]
    heads = shape[3] // HEAD_DIM
    cut = (heads + 1) // 2 if heads > 1 else heads
    parts = [(low, high) for low, high in ((0, cut), (cut, heads)) if high > low]
    owns, ends, mids, fars = [], [], [], []
    for low, high in parts:
        lanes = slice(low * HEAD_DIM, high * HEAD_DIM)
        own = jnp.concatenate(
            [block[0, :, :, lanes].reshape(tokens, -1) for block in (keys, values)], 0
        )
        ends.append(moved(own, inward))
        mids.append(moved(own, across))
        owns.append([own, swapped(own)])
        fars.append(moved(ends[-1], across))
    marks = jnp.broadcast_to(valid_prev[0][:, None], (shape[1], shape[3])).astype(jnp.bfloat16)
    marks = jnp.pad(marks, ((0, 16 - shape[1]), (0, 0)))
    end_query = moved(jnp.concatenate([query, marks], 0), inward)
    mids = [[mid, swapped(mid)] for mid in mids]
    ends = [[end, swapped(end)] for end in ends]
    memory = marker(mem_index)
    end_states = [
        attend(
            functools.partial(plan_four, 1, (0, 1, 2)),
            (True, False, False),
            memory,
            valid_prev,
            end_query,
            low,
            [own, mid, end],
            None,
            False,
            width,
            SHORT,
            marked=True,
        )
        for (low, _), own, mid, end in zip(parts, owns, mids, ends)
    ]
    backs = []
    token = end_states[-1][1]
    for n, (low, _) in enumerate(parts):
        far, token = lax.optimization_barrier((fars[n], token))
        if n == 0:
            end_states[-1][1] = token
        fars[n] = [far, swapped(far)]
        back, token = attend(
            functools.partial(plan_four, 1, (3,)),
            (False,),
            memory if n == 0 else token,
            valid_prev,
            end_query,
            low,
            [fars[n]],
            end_states[n],
            True,
            width,
            SHORT,
        )
        backs.append(back)
    backs = [moved(back, [(1, 0), (2, 3)]) for back in backs]
    outs = [
        attend(
            functools.partial(plan_four, 0, (0, 1, 2, 3)),
            (False, True, True, False),
            memory,
            valid_prev,
            query,
            low,
            frames,
            None,
            True,
            width,
            LONG,
        )[0]
        for (low, _), *frames in zip(parts, owns, mids, ends, fars)
    ]
    z = lax.axis_index("frame")
    middle = (z == 1) | (z == 2)
    out = [jnp.where(middle, out, back) for out, back in zip(outs, backs)]
    return jnp.concatenate(out, 1).reshape(shape)


def any_frames(queries, keys, values, valid_prev, mem_index):
    shape = queries.shape
    width = shape[2]
    tokens = shape[1] * width
    count = lax.axis_size("frame")
    z = lax.axis_index("frame")

    def flat(block):
        return block.reshape(tokens, shape[3])

    own = jnp.concatenate([flat(keys), flat(values)], 0)
    before = moved(own, [(i, i + 1) for i in range(count - 1)])
    masked = jnp.stack([jnp.where(z == mem_index[s], own, jnp.zeros_like(own)) for s in range(2)])
    memory = lax.psum(masked, "frame")
    out, _ = attend(
        plan_any,
        (False, True, False, False),
        mem_index,
        valid_prev,
        flat(queries),
        0,
        [[kv, swapped(kv)] for kv in (own, before, memory[0], memory[1])],
        None,
        True,
        width,
        LONG,
    )
    return out.reshape(shape)


def solution(mesh):
    spread = P(("groups", "frame"), "row", None, "head")
    body = four_frames if mesh.shape["frame"] == 4 else any_frames
    return jax.shard_map(
        body,
        mesh=mesh,
        in_specs=(spread, spread, spread, P(("groups", "frame"), "row"), P("groups")),
        out_specs=spread,
        check_vma=False,
    )
```

```python
import functools

import jax
import jax.numpy as jnp
from jax import lax
from jax.experimental import pallas as pl
from jax.experimental.pallas import tpu as pltpu
from jax.sharding import PartitionSpec as P

HEAD_DIM = 128
WINDOW = 2
SCALE = HEAD_DIM**-0.5 * 1.4426950408889634
FLOOR = -1e30
BLOCK = 128
LOG2_3 = 1.584962500721156
LONG = 20_000_000_000
SHORT = 1000


def moved(block, pairs):
    return lax.ppermute(block, "frame", pairs)


def swapped(block):
    return lax.ppermute(block, "row", [(0, 1), (1, 0)])


def log2_weight(count):
    return jnp.where(
        count < 1, -jnp.inf, jnp.where(count < 2, 0.0, jnp.where(count < 3, 1.0, LOG2_3))
    ).astype(jnp.float32)


def attend_kernel(plan, windows, marked, n_f, fresh, finish, width, *refs):
    refs = list(refs)
    mem_ref, valid_ref, q_ref = refs[:3]
    frames = [refs[3 + 2 * f : 5 + 2 * f] for f in range(n_f)]
    n_in = 3 + 2 * n_f + (0 if fresh else 2)
    acc, peaks = refs[n_in + 2 - finish : n_in + 4 - finish]
    lane = lax.broadcasted_iota(jnp.int32, (1, HEAD_DIM), 1)
    queries, channels = frames[0][0].shape
    queries //= 2
    heads = channels // HEAD_DIM
    rows = queries // width
    band = lax.axis_index("row")
    z = lax.axis_index("frame")

    acc[...] = jnp.zeros_like(acc)
    peaks[...] = jnp.full(peaks.shape, FLOOR, jnp.float32)
    if not fresh:
        total, stat, sems = refs[-3:]
        copies = [
            pltpu.make_async_copy(refs[n_in - 2 + n], buf, sems.at[n])
            for n, buf in enumerate((total, stat))
        ]
        for copy in copies:
            copy.start()
    ones = jnp.ones((2 * queries, HEAD_DIM), jnp.bfloat16)

    def step(f, times, window):
        factor = times.astype(jnp.float32)
        if window:
            outside, inside = log2_weight(times), log2_weight(times + 1)
            if marked:
                marks = q_ref[pl.ds(queries, 16), 0:HEAD_DIM].astype(jnp.float32)
            place = lax.broadcasted_iota(jnp.int32, (1, 2 * queries), 1)
            key_row = jnp.zeros((1, 2 * queries), jnp.int32)
            for r in range(1, 2 * rows):
                key_row = key_row + (place >= r * width).astype(jnp.int32)
            key_row = jnp.where(
                key_row < rows, key_row + band * rows, key_row - rows + (1 - band) * rows
            )
        for start in range(0, queries, BLOCK):
            part = pl.ds(start, BLOCK)
            if window:
                place = lax.broadcasted_iota(jnp.int32, (BLOCK, 1), 0) + start
                row = jnp.full((BLOCK, 1), -1000, jnp.int32)
                for r in range(rows):
                    here = (place >= r * width) & (place < (r + 1) * width)
                    if marked:
                        here = here & (marks[r : r + 1, 0:1] > 0.0)
                    else:
                        here = here & (valid_ref[0, r] > 0)
                    row = jnp.where(here, band * rows + r, row)
                bias = jnp.where(jnp.abs(key_row - row) <= WINDOW, inside, outside)
            for h in range(heads):
                lanes = pl.ds(h * HEAD_DIM, HEAD_DIM)
                key, value = [
                    jnp.concatenate([half[pl.ds(n * queries, queries), lanes] for half in frames[f]], 0)
                    for n in range(2)
                ]
                scores = (
                    lax.dot_general(
                        q_ref[part, lanes],
                        key,
                        (((1,), (1,)), ((), ())),
                        preferred_element_type=jnp.float32,
                    )
                    * SCALE
                )
                if window:
                    scores = scores + bias
                old = peaks[h, part, :]
                peak = jnp.maximum(old, jnp.max(scores, axis=1, keepdims=True))
                terms = jnp.exp2(scores - peak[:, 0:1]).astype(jnp.bfloat16)
                mixed = jnp.dot(
                    terms,
                    jnp.concatenate([value, ones], 1),
                    preferred_element_type=jnp.float32,
                )
                if not window:
                    mixed = mixed * factor
                fade = jnp.exp2(old - peak)
                acc[h, part, :] = acc[h, part, :] * jnp.concatenate([fade, fade], 1) + mixed
                peaks[h, part, :] = peak

    for f in range(n_f):
        times, window = plan(z, mem_ref[0], mem_ref[1], f)
        if windows[f]:
            pl.when(window)(functools.partial(step, f, times, True))
            pl.when((times > 0) & jnp.logical_not(window))(
                functools.partial(step, f, times, False)
            )
        else:
            pl.when(times > 0)(functools.partial(step, f, times, False))

    if not fresh:
        for copy in copies:
            copy.wait()
        for h in range(heads):
            shape = (queries, HEAD_DIM)
            old = jnp.broadcast_to(stat[:, h : h + 1], shape)
            weight = jnp.broadcast_to(stat[:, heads + h : heads + h + 1], shape)
            peak = jnp.maximum(old, peaks[h])
            fade, scale = jnp.exp2(peaks[h] - peak), jnp.exp2(old - peak)
            acc[h, :, :HEAD_DIM] = (
                acc[h, :, :HEAD_DIM] * fade + total[:, pl.ds(h * HEAD_DIM, HEAD_DIM)] * scale
            )
            acc[h, :, HEAD_DIM:] = acc[h, :, HEAD_DIM:] * fade + weight * scale
            peaks[h] = peak

    if finish:
        out = refs[n_in]
        for h in range(heads):
            out[:, pl.ds(h * HEAD_DIM, HEAD_DIM)] = (
                acc[h, :, :HEAD_DIM] / acc[h, :, HEAD_DIM:]
            ).astype(jnp.bfloat16)
    else:
        total, stat = refs[n_in : n_in + 2]
        packed = jnp.zeros((queries, HEAD_DIM), jnp.float32)
        for h in range(heads):
            total[:, pl.ds(h * HEAD_DIM, HEAD_DIM)] = acc[h, :, :HEAD_DIM]
            packed = jnp.where(lane == h, peaks[h], packed)
            packed = jnp.where(lane == heads + h, acc[h, :, HEAD_DIM:], packed)
        stat[...] = packed


def attend(
    plan, windows, mem_index, valid, query, frames, state, finish, width, cost, marked=False
):
    tokens, channels = frames[0][0].shape
    tokens //= 2
    heads = channels // HEAD_DIM
    scalars = pl.BlockSpec(memory_space=pltpu.SMEM)
    whole = pl.BlockSpec(memory_space=pltpu.VMEM)
    operands = [mem_index, valid, query]
    for frame in frames:
        operands += frame
    if state is not None:
        operands += [pltpu.with_memory_space_constraint(s, pltpu.HBM) for s in state]
    shapes = [jax.ShapeDtypeStruct((tokens, channels), jnp.bfloat16)]
    if not finish:
        shapes = [
            jax.ShapeDtypeStruct((tokens, channels), jnp.float32),
            jax.ShapeDtypeStruct((tokens, HEAD_DIM), jnp.float32),
        ]
    scratch = [
        pltpu.VMEM((heads, tokens, 2 * HEAD_DIM), jnp.float32),
        pltpu.VMEM((heads, tokens, HEAD_DIM), jnp.float32),
    ]
    specs = [scalars] * 2 + [whole] * (1 + 2 * len(frames))
    if state is not None:
        specs += [pl.BlockSpec(memory_space=pltpu.HBM)] * 2
        scratch += [pltpu.VMEM(s.shape, s.dtype) for s in state]
        scratch.append(pltpu.SemaphoreType.DMA((2,)))
    outs = pl.pallas_call(
        functools.partial(
            attend_kernel,
            plan,
            windows,
            marked,
            len(frames),
            state is None,
            finish,
            width,
        ),
        in_specs=specs,
        out_specs=[whole] * len(shapes),
        out_shape=shapes,
        scratch_shapes=scratch,
        compiler_params=pltpu.CompilerParams(vmem_limit_bytes=16 << 20),
        cost_estimate=pl.CostEstimate(flops=cost, transcendentals=0, bytes_accessed=1000),
    )(*operands)
    return outs[0] if finish else list(outs)


def marker(valid):
    def kernel(valid_ref, out_ref):
        for n in range(valid_ref.shape[1]):
            out_ref[0, n] = valid_ref[0, n]

    scalars = pl.BlockSpec(memory_space=pltpu.SMEM)
    return pl.pallas_call(
        kernel,
        in_specs=[scalars],
        out_specs=scalars,
        out_shape=jax.ShapeDtypeStruct(valid.shape, jnp.int32),
        cost_estimate=pl.CostEstimate(flops=LONG, transcendentals=0, bytes_accessed=1000),
    )(valid)


def plan_four(query_set, names, z, first, second, f):
    middle = (z == 1) | (z == 2)
    ids = (z, 3 - z, 3 * (z - 1), 6 - 3 * z)
    mine, frame = ids[2 * query_set], ids[names[f]]
    times = (
        (frame == mine).astype(jnp.int32)
        + (first == frame).astype(jnp.int32)
        + (second == frame).astype(jnp.int32)
    )
    return jnp.where(middle, times, 0), middle & (frame == mine - 1)


def plan_any(z, first, second, f):
    return jnp.int32(0 if f == 1 else 1), z > 0


def four_frames(queries, keys, values, valid_prev, mem_index):
    shape = queries.shape
    width = shape[2]
    tokens = shape[1] * width

    def flat(block):
        return block.reshape(tokens, shape[3])

    query = flat(queries)
    inward = [(0, 1), (3, 2)]
    across = [(1, 2), (2, 1)]
    own = jnp.concatenate([flat(keys), flat(values)], 0)
    end = moved(own, inward)
    mid = moved(own, across)
    own = [own, swapped(own)]
    far = moved(end, across)
    marks = jnp.broadcast_to(valid_prev[0][:, None], (shape[1], shape[3])).astype(jnp.bfloat16)
    marks = jnp.pad(marks, ((0, 16 - shape[1]), (0, 0)))
    end_query = moved(jnp.concatenate([query, marks], 0), inward)
    mid = [mid, swapped(mid)]
    end = [end, swapped(end)]
    end_state = attend(
        functools.partial(plan_four, 1, (0, 1, 2)),
        (True, False, False),
        mem_index,
        marker(valid_prev),
        end_query,
        [own, mid, end],
        None,
        False,
        width,
        SHORT,
        marked=True,
    )
    far, end_state = lax.optimization_barrier((far, end_state))
    far = [far, swapped(far)]
    end_out = attend(
        functools.partial(plan_four, 1, (3,)),
        (False,),
        mem_index,
        valid_prev,
        end_query,
        [far],
        end_state,
        True,
        width,
        SHORT,
    )
    back = moved(end_out, [(1, 0), (2, 3)])
    out = attend(
        functools.partial(plan_four, 0, (0, 1, 2, 3)),
        (False, True, True, False),
        mem_index,
        valid_prev,
        query,
        [own, mid, end, far],
        None,
        True,
        width,
        LONG,
    )
    z = lax.axis_index("frame")
    return jnp.where((z == 1) | (z == 2), out, back).reshape(shape)


def any_frames(queries, keys, values, valid_prev, mem_index):
    shape = queries.shape
    width = shape[2]
    tokens = shape[1] * width
    count = lax.axis_size("frame")
    z = lax.axis_index("frame")

    def flat(block):
        return block.reshape(tokens, shape[3])

    own = jnp.concatenate([flat(keys), flat(values)], 0)
    before = moved(own, [(i, i + 1) for i in range(count - 1)])
    masked = jnp.stack([jnp.where(z == mem_index[s], own, jnp.zeros_like(own)) for s in range(2)])
    memory = lax.psum(masked, "frame")
    out = attend(
        plan_any,
        (False, True, False, False),
        mem_index,
        valid_prev,
        flat(queries),
        [[kv, swapped(kv)] for kv in (own, before, memory[0], memory[1])],
        None,
        True,
        width,
        LONG,
    )
    return out.reshape(shape)


def solution(mesh):
    spread = P(("groups", "frame"), "row", None, "head")
    body = four_frames if mesh.shape["frame"] == 4 else any_frames
    return jax.shard_map(
        body,
        mesh=mesh,
        in_specs=(spread, spread, spread, P(("groups", "frame"), "row"), P("groups")),
        out_specs=spread,
        check_vma=False,
    )
```
